1024 devices in a mesh: grp: 2 (over y_hi), reg: 32 (over z, y_lo), sub: 16 (over x, core).
Axes of the slice: x: 8, y: 8 (y_hi: 2, y_lo: 4; y = y_hi * 4 + y_lo), z: 8, core: 2. Of those that a mesh axis runs over, the one named last changes fastest.
Arguments:
- column_state: float32 [2, 128, 262144], P('grp', None, ('reg', 'sub')), may hold values from -6 to 6
- neighbours: int32 [2, 3, 262144], P('grp', None, ('reg', 'sub')), may hold values from 0 to 1055, as said below
- mixing: float32 [2, 128, 128], P('grp'), may hold values from -0.109375 to 0.109375
- diffusivity: float32 [2, 128], P('grp'), may hold values from 0.03 to 0.3
- flux_map: float32 [4, 128], replicated, may hold values from -0.625 to 0.625
- force_map: float32 [128, 4], replicated, may hold values from -3 to 3
- return_map: float32 [3, 128], replicated, may hold values from -0.5 to 0.5
- sources: int32 [3, 262144], P(None, ('reg', 'sub')), may hold values from 0 to 8191
- remap_weights: float32 [3, 262144], P(None, ('reg', 'sub')), may hold values from 0.1 to 0.6
- wet: int32 [262144], P(('reg', 'sub')), may hold values 0 or 1
Outputs:
- new_state: float32 [2, 128, 262144], P('grp', None, ('reg', 'sub'))
- coupled_surface: float32 [3, 262144], P(None, ('reg', 'sub'))
The draws below stay inside these ranges and needn't reach their ends.
Inputs may be any that keep to these rules, and one draw needn't show every extreme that they name: A cell's neighbours lie within 2 rows and 2 columns of it in its extended patch. sources point into the ocean cell's own slab.
All inputs are finite; a program needn't handle non-finite values. No bound on the sum of `wet` on one device may be relied on, other than what follows from the above.
Results may differ from the reference program's by a relative error of at most 0.0001.
Values sent between devices are 32-bit elements; how exact they have to be, the bound alone decides.
A program may use at most 64 MiB of HBM per device.

```python
import math
import jax
import jax.numpy as jnp
from jax import lax

LEV = 128
LA = 90
CELLS = 512
BS = 128
HALO = 2
STEPS = 4
LINKS = 3
NF = 4
NR = 3
CELLS_ALL = 262144
N_REG = 32
N_SUB = 16


def draw_neighbours(key, part):
    place = jnp.arange(CELLS_ALL, dtype=jnp.int32) % CELLS
    prow = place // BS
    pcol = place % BS
    key_row = jax.random.fold_in(key, 11)
    key_col = jax.random.fold_in(key, 23)
    drow = jax.random.randint(key_row, (2, LINKS, CELLS_ALL), -HALO, HALO + 1, dtype=jnp.int32)
    dcol = jax.random.randint(key_col, (2, LINKS, CELLS_ALL), -HALO, HALO + 1, dtype=jnp.int32)
    index = (prow[None, None, :] + HALO + drow) * (BS + 2 * HALO) + (pcol[None, None, :] + HALO + dcol)
    return index.astype(jnp.int32)


def with_ends(drawn, rng, least, largest):
    longest = drawn.shape.index(max(drawn.shape))
    spots = []
    for shift in (0, 1):
        where = [jax.random.randint(jax.random.fold_in(rng, axis), (), 0, length) for axis, length in enumerate(drawn.shape)]
        where[longest] = (where[longest] + shift) % drawn.shape[longest]
        spots.append(tuple(where))
    return drawn.at[spots[0]].set(least).at[spots[1]].set(largest)


def shard_levels(key, extent, pieces, least, largest):
    def one(position, shards_of):
        steps = jax.random.uniform(jax.random.fold_in(jax.random.fold_in(key, 6), position), (shards_of,), jnp.float32, least / len(pieces), largest / len(pieces))
        return jnp.repeat(jnp.exp(steps), extent[position] // shards_of).reshape((-1,) + (1,) * (len(extent) - position - 1))

    gain = one(*pieces[0])
    for cut in pieces[1:]:
        gain = gain * one(*cut)
    return gain


def noise(own_key, extent, deviation, reach, shards=(), held_as=jnp.bfloat16):
    factor_of = shard_levels(own_key, extent, shards, -0.22, 0.18) if shards else 1.0
    array = jax.random.normal(own_key, extent, jnp.float32) * deviation * factor_of
    return jnp.minimum(jnp.maximum(array, -reach), reach).astype(held_as)


def setup_inputs(seed: int = 0) -> dict:
    seeds = jax.random.split(jax.random.key(seed), 11)
    column_state = noise(seeds[0], (2, LEV, CELLS_ALL), 1.0, 6.0, ((0, 2), (2, 512)), jnp.float32)
    neighbours = draw_neighbours(jax.random.fold_in(seeds[10], 71), 0)
    mixing = noise(seeds[2], (2, LEV, LEV), (25 * LEV) ** -0.5, 0.109375, ((0, 2),), jnp.float32)
    diffusivity = jnp.clip(jnp.exp(math.log(0.3) - 2.3025852 * jax.random.uniform(seeds[3], (2, LEV), jnp.float32) ** shard_levels(seeds[3], (2, LEV), ((0, 2),), -0.2, 0.2)), 0.03, 0.3)
    flux_map = noise(seeds[4], (NF, LEV), LA ** -0.5, 0.625, (), jnp.float32)
    force_map = noise(seeds[5], (LEV, NF), NF ** -0.5, 3.0, (), jnp.float32)
    return_map = noise(seeds[6], (NR, LEV), LEV ** -0.5, 0.5, (), jnp.float32)
    sources = with_ends(jax.random.randint(seeds[7], (LINKS, CELLS_ALL), 0, N_SUB * CELLS), jax.random.fold_in(seeds[7], 1), 0, (N_SUB * CELLS) - 1).astype(jnp.int32)
    remap_weights = jnp.clip(0.1 + 0.5 * jax.random.uniform(seeds[8], (LINKS, CELLS_ALL), jnp.float32) ** shard_levels(seeds[8], (LINKS, CELLS_ALL), ((1, 512),), -0.2, 0.2), 0.1, 0.6)
    wet = with_ends((jax.random.randint(seeds[9], (CELLS_ALL,), 0, 3) < 2).astype(jnp.int32), jax.random.fold_in(seeds[9], 1), 0, 1)
    return {"column_state": column_state, "neighbours": neighbours, "mixing": mixing, "diffusivity": diffusivity, "flux_map": flux_map, "force_map": force_map, "return_map": return_map, "sources": sources, "remap_weights": remap_weights, "wet": wet}


def extend(field):
    levels = field.shape[0]
    rows = CELLS // BS
    grid = field.reshape(levels, N_REG, N_SUB, rows, BS).transpose(0, 1, 3, 2, 4)
    grid = grid.reshape(levels, N_REG * rows, N_SUB * BS)
    return jnp.pad(grid, ((0, 0), (HALO, HALO), (HALO, HALO)), mode="wrap")


def spread(field, links, rate):
    rows = CELLS // BS
    padded = extend(field)
    cell = jnp.arange(CELLS_ALL, dtype=jnp.int32)
    slab = cell // (N_SUB * CELLS)
    block = (cell // CELLS) % N_SUB
    total = -float(LINKS) * field
    for k in range(LINKS):
        index = links[k].astype(jnp.int32)
        erow = index // (BS + 2 * HALO)
        ecol = index % (BS + 2 * HALO)
        taken = padded[:, slab * rows + erow, block * BS + ecol]
        total = total + taken
    return field + rate[:, None] * total


def mix(field, matrix):
    return field + jnp.dot(matrix, field, precision=lax.Precision.HIGHEST, preferred_element_type=jnp.float32)


def slab_targets(sources):
    cell = jnp.arange(CELLS_ALL, dtype=jnp.int32)
    base = (cell // (N_SUB * CELLS)) * (N_SUB * CELLS)
    return (base[None, :] + sources).astype(jnp.int32)


def reference(column_state, neighbours, mixing, diffusivity, flux_map, force_map, return_map, sources, remap_weights, wet):
    levels = jnp.arange(LEV, dtype=jnp.int32)[:, None]
    keep = (levels < LA).astype(jnp.float32)
    atmos = column_state[0] * keep
    flux = jnp.zeros((NF, CELLS_ALL), jnp.float32)
    for step in range(STEPS):
        atmos = keep * mix(spread(atmos, neighbours[0], diffusivity[0]), mixing[0])
        flux = flux + jnp.dot(flux_map, atmos, precision=lax.Precision.HIGHEST, preferred_element_type=jnp.float32)
    flux = flux / float(STEPS)
    targets = slab_targets(sources)
    ocean_flux = jnp.zeros((NF, CELLS_ALL), jnp.float32)
    for k in range(LINKS):
        ocean_flux = ocean_flux + remap_weights[k][None, :] * flux[:, targets[k]]
    wet_cells = wet.astype(jnp.float32)[None, :]
    start = column_state[1]
    pushed = spread(start, neighbours[1], diffusivity[1]) + jnp.dot(force_map, ocean_flux, precision=lax.Precision.HIGHEST, preferred_element_type=jnp.float32)
    ocean = start + wet_cells * (mix(pushed, mixing[1]) - start)
    new_state = jnp.stack([atmos, ocean], axis=0)
    surface = jnp.dot(return_map, ocean, precision=lax.Precision.HIGHEST, preferred_element_type=jnp.float32) * wet_cells
    coupled = jnp.zeros((NR, CELLS_ALL), jnp.float32)
    for k in range(LINKS):
        coupled = coupled.at[:, targets[k]].add(remap_weights[k][None, :] * surface)
    return new_state, coupled
```

```python
import jax
import jax.numpy as jnp
from jax import lax
from jax.experimental import pallas as pl
from jax.experimental.pallas import tpu as pltpu
from jax.sharding import PartitionSpec as P

LA = 90
LEV = 128
CELLS = 512
BS = 128
STEPS = 4
RUN = 4
COLS = 32
ROWS = 16
SLOTS = 768
EXT = BS + 4
MESH = pl.DeviceIdType.MESH
F32 = jnp.float32
BF16 = jnp.bfloat16


def exact_dot(a, b, dims):
    return lax.dot_general(
        a, b, (dims, ((), ())), precision=lax.Precision.HIGHEST, preferred_element_type=F32
    )


def fast_dot(a, b, dims):
    return lax.dot_general(a, b, (dims, ((), ())), preferred_element_type=F32)


NN = ((1,), (0,))
NT = ((1,), (1,))


def pieces(x):
    high = x.astype(BF16)
    return high, (x - high.astype(F32)).astype(BF16)


def rows8(x):
    return jnp.concatenate([x, jnp.zeros((8 - x.shape[0], x.shape[1]), x.dtype)], axis=0)


def iota(shape, dim):
    return lax.broadcasted_iota(jnp.int32, shape, dim)


def lane_roll(x, shift):
    shift = shift % x.shape[1]
    return x if shift == 0 else pltpu.roll(x, shift, 1)


def regroup(parts, n):
    width = parts[0].shape[1] // n
    group = iota(parts[0].shape, 1) // width
    out = []
    for b in range(n):
        total = lane_roll(parts[0], -b * width)
        for a in range(1, n):
            total = jnp.where(group == a, lane_roll(parts[a], (a - b) * width), total)
        out.append(total)
    return out


def body(
    n_zone,
    n_sub,
    cs_in,
    nb_in,
    mix_in,
    rate_in,
    fm_in,
    force_in,
    rm_in,
    src_in,
    rw_in,
    wet_in,
    ns_out,
    cpl_out,
    start,
    nb,
    mixing,
    rate,
    fm,
    force,
    rm,
    src,
    rw,
    wet,
    vt,
    idq,
    nidx,
    cnt,
    vx,
    edge,
    vsum,
    w2,
    oh,
    fx,
    fin,
    ft,
    ftab,
    rt,
    bmsg,
    bin_,
    pbuf,
    cin,
    nsb,
    cplb,
    in_sem,
    t_send,
    t_recv,
    h_send,
    h_recv,
    f_send,
    f_recv,
    r_send,
    r_recv,
    x_send,
    x_recv,
    b_send,
    b_recv,
    o_sem,
):
    grp = lax.axis_index("grp")
    reg = lax.axis_index("reg")
    s = lax.axis_index("sub")
    z = reg // RUN
    j = reg % RUN
    odd = s % 2
    ocean = grp == 1
    atmos = grp == 0

    def chunk_of(place):
        return jnp.where(odd == 1, RUN - 1 - place, place)

    q = chunk_of(j)
    z_up = lax.rem(z + n_zone - 1, n_zone)
    z_down = lax.rem(z + 1, n_zone)
    s_before = lax.rem(s + n_sub - 1, n_sub)
    s_after = lax.rem(s + 1, n_sub)
    l_j = jnp.where(q == 0, j, chunk_of(q - 1))
    l_s = jnp.where(q == 0, s_before, s)
    r_j = jnp.where(q == RUN - 1, j, chunk_of(q + 1))
    r_s = jnp.where(q == RUN - 1, s_after, s)

    def at(g, zone, place, sub):
        return (g, zone * RUN + place, sub)

    run_peers = [lax.rem(j + d, RUN) for d in range(RUN)]
    sub_peers = [lax.rem(s + d, n_sub) for d in range(n_sub)]
    halo_peers = [
        at(grp, z_up, j, s),
        at(grp, z_down, j, s),
        at(grp, z, l_j, l_s),
        at(grp, z, r_j, r_s),
        at(grp, z_up, l_j, l_s),
        at(grp, z_up, r_j, r_s),
        at(grp, z_down, l_j, l_s),
        at(grp, z_down, r_j, r_s),
    ]

    barrier = pltpu.get_barrier_semaphore()
    greeted = [at(grp, z, p, s) for p in run_peers[1:]]
    greeted += [at(1 - grp, z, p, s) for p in run_peers]
    greeted += [at(grp, z, j, p) for p in sub_peers[1:]]
    greeted += halo_peers
    for device in greeted:
        pl.semaphore_signal(barrier, inc=1, device_id=device, device_id_type=MESH)

    loads = [
        pltpu.make_async_copy(a, b, in_sem.at[n])
        for n, (a, b) in enumerate(
            [
                (cs_in.at[0], start),
                (nb_in, nb),
                (mix_in.at[0], mixing),
                (rate_in, rate),
                (fm_in, fm),
                (force_in, force),
                (rm_in, rm),
                (src_in, src),
                (rw_in, rw),
                (wet_in, wet),
            ]
        )
    ]
    for load in loads:
        load.start()

    lane = iota((1, LEV), 1)
    keep = jnp.logical_or(lane < LA, ocean).astype(F32)

    loads[1].wait()
    lanes_rq = [
        rows8(jnp.concatenate([nb[k, :, pl.ds(r * BS, BS)] for k in range(3)], axis=0))
        for r in range(RUN)
    ]
    for c, block in enumerate(regroup(lanes_rq, RUN)):
        idq[c] = block

    loads[0].wait()
    for r in range(RUN):
        vt[r] = jnp.transpose(start[:, r * BS : (r + 1) * BS]) * keep

    pl.semaphore_wait(barrier, len(greeted))

    def remote(source, target, send, recv, device):
        return pltpu.make_async_remote_copy(
            src_ref=source,
            dst_ref=target,
            send_sem=send,
            recv_sem=recv,
            device_id=device,
            device_id_type=MESH,
        )

    index_copies, state_copies = [], []
    for d in range(1, RUN):
        peer = run_peers[d]
        c = chunk_of(peer)
        index_copies.append(
            remote(idq.at[c], nidx.at[j], t_send.at[0, d], t_recv.at[0, d], at(grp, z, peer, s))
        )
        state_copies.append(
            remote(
                vt.at[:, pl.ds(pl.multiple_of(c * COLS, COLS), COLS), :],
                vx.at[0, pl.ds(j * RUN, RUN)],
                t_send.at[1, d],
                t_recv.at[1, d],
                at(grp, z, peer, s),
            )
        )
    for copy in index_copies + state_copies:
        copy.start()
    nidx[j] = idq[q]
    for r in range(RUN):
        vx[0, j * RUN + r] = vt[r, pl.ds(pl.multiple_of(q * COLS, COLS), COLS), :]
    for n in range(STEPS):
        vx[n, 23] = jnp.zeros((COLS, LEV), F32)
    vsum[...] = jnp.zeros_like(vsum)

    loads[2].wait()
    m_high, m_low = pieces(jnp.transpose(mixing[...]))
    for a in range(2):
        w2[a * LEV : (a + 1) * LEV, 0:LEV] = m_high
        w2[a * LEV : (a + 1) * LEV, LEV : 2 * LEV] = m_low

    loads[7].wait()
    place = src[...]
    owner = (place // CELLS) * RUN + (place % BS) // COLS
    inside = ((place % CELLS) // BS) * COLS + place % COLS
    for k in range(3):
        hot = (iota((BS, CELLS), 0) == inside[k : k + 1, :]).astype(F32).astype(BF16)
        oh[0:BS, k * CELLS : (k + 1) * CELLS] = hot
        oh[BS : 2 * BS, k * CELLS : (k + 1) * CELLS] = hot

    for copy in index_copies:
        copy.wait_recv()
    for i in range(RUN):
        link = nidx[i]
        e_row = jnp.zeros_like(link)
        for a in range(1, 8):
            e_row = e_row + (link >= a * EXT).astype(jnp.int32)
        row = e_row + (i * RUN - 2)
        col = link - e_row * EXT - 2 - q * COLS
        above, below = row < 0, row >= ROWS
        left, right = col < 0, col >= COLS
        slot = row * COLS + col
        slot = jnp.where(above, (row + 2) * COLS + col + 512, slot)
        slot = jnp.where(below, (row - ROWS) * COLS + col + 576, slot)
        slot_l = row * 2 + col + 642
        slot_l = jnp.where(above, (row + 4) * 2 + col + 706, slot_l)
        slot_l = jnp.where(below, (row - ROWS) * 2 + col + 722, slot_l)
        slot_r = row * 2 + col - COLS + 672
        slot_r = jnp.where(above, (row + 4) * 2 + col - COLS + 712, slot_r)
        slot_r = jnp.where(below, (row - ROWS) * 2 + col - COLS + 728, slot_r)
        slot = jnp.where(left, slot_l, jnp.where(right, slot_r, slot)).astype(F32)
        tall = jnp.concatenate([slot, jnp.zeros((BS - 8, BS), F32)], axis=0)
        slot_t = jnp.transpose(tall)
        for b in range(SLOTS // BS):
            here = (iota((BS, BS), 1) + b * BS).astype(F32)
            total = (slot_t[:, 0:1] == here).astype(F32)
            for k in range(1, 3):
                total = total + (slot_t[:, k : k + 1] == here).astype(F32)
            cnt[i * BS : (i + 1) * BS, b * BS : (b + 1) * BS] = total.astype(BF16)

    loads[3].wait()
    for copy in state_copies:
        copy.wait_recv()

    def step(n, carry):
        for row in range(ROWS):
            spot = pl.ds(2 * (row % 4), 2)
            edge[n, 0, row // 4, spot, :] = vx[n, row, 0:2, :]
            edge[n, 1, row // 4, spot, :] = vx[n, row, COLS - 2 : COLS, :]
        routes = [
            (vx.at[n, pl.ds(0, 2)], vx.at[n, pl.ds(18, 2)]),
            (vx.at[n, pl.ds(14, 2)], vx.at[n, pl.ds(16, 2)]),
            (edge.at[n, 0], vx.at[n, 21]),
            (edge.at[n, 1], vx.at[n, 20]),
            (edge.at[n, 0, 0], vx.at[n, 22, pl.ds(24, 8)]),
            (edge.at[n, 1, 0], vx.at[n, 22, pl.ds(16, 8)]),
            (edge.at[n, 0, 3], vx.at[n, 22, pl.ds(8, 8)]),
            (edge.at[n, 1, 3], vx.at[n, 22, pl.ds(0, 8)]),
        ]
        copies = []
        for d, (source, target) in enumerate(routes):
            if d in (2, 3):
                for part in range(4):
                    copies.append(
                        remote(
                            source.at[part],
                            target.at[pl.ds(8 * part, 8)],
                            h_send.at[n, d * 4 + part],
                            h_recv.at[n, d * 4 + part],
                            halo_peers[d],
                        )
                    )
            else:
                copies.append(
                    remote(source, target, h_send.at[n, d], h_recv.at[n, d], halo_peers[d])
                )
        for copy in copies:
            copy.start()
        field = vx[n, 0:ROWS].reshape(CELLS, LEV)
        high, low = pieces(field)
        acc = fast_dot(cnt[:, 0:CELLS], jnp.concatenate([high, low], axis=1), NN)
        for copy in copies:
            copy.wait_recv()
        high, low = pieces(vx[n, ROWS:24].reshape(SLOTS - CELLS, LEV))
        acc = acc + fast_dot(cnt[:, CELLS:SLOTS], jnp.concatenate([high, low], axis=1), NN)
        total = acc[:, 0:LEV] + acc[:, LEV : 2 * LEV]
        spread = field + rate[...] * (total - 3.0 * field)
        high, low = pieces(spread)
        mixed = fast_dot(jnp.concatenate([high, low], axis=1), w2[...], NN)
        new = keep * (spread + mixed[:, 0:LEV] + mixed[:, LEV : 2 * LEV])
        vx[n + 1, 0:ROWS] = new.reshape(ROWS, COLS, LEV)
        vsum[...] = vsum[...] + new
        for copy in copies:
            copy.wait_send()
        return carry

    n_steps = jnp.where(ocean, 1, STEPS)
    lax.fori_loop(0, n_steps, step, 0)

    def flux_copies(g):
        return [
            remote(
                fx.at[i],
                fin.at[q],
                f_send.at[g, i],
                f_recv.at[j],
                at(g, z, i, s),
            )
            for i in range(RUN)
        ]

    loads[4].wait()

    @pl.when(atmos)
    def _():
        flux = exact_dot(rows8(fm[...]), vsum[...], NT) * (1.0 / STEPS)
        for i in range(RUN):
            fx[i] = flux[:, i * BS : (i + 1) * BS]
        for i, copy in enumerate(flux_copies(0)):

            @pl.when(j != i)
            def _(copy=copy):
                copy.start()

        for copy in flux_copies(1):
            copy.start()
        fin[q] = fx[j]

    last = n_steps
    back_copies = []
    for d in range(1, RUN):
        peer = run_peers[d]
        back_copies.append(
            remote(
                vx.at[last, pl.ds(peer * RUN, RUN)],
                rt.at[:, pl.ds(pl.multiple_of(q * COLS, COLS), COLS), :],
                r_send.at[d],
                r_recv.at[d],
                at(grp, z, peer, s),
            )
        )
    for copy in back_copies:
        copy.start()
    for r in range(RUN):
        rt[r, pl.ds(pl.multiple_of(q * COLS, COLS), COLS), :] = vx[last, j * RUN + r]

    loads[5].wait()
    loads[6].wait()
    loads[8].wait()
    loads[9].wait()
    to_atmos = remote(bmsg, bin_, b_send, b_recv, at(1 - grp, z, j, s))
    force_t = rows8(force[...])
    pushed_t = force_t + exact_dot(force_t, mixing[...], NT)

    @pl.when(ocean)
    def _():
        for copy in back_copies:
            copy.wait_recv()
        returns = rows8(rm[...])
        base = exact_dot(returns, rt[...].reshape(CELLS, LEV), NT)
        gains = jnp.zeros((8, BS), F32)
        for f in range(4):
            gain = jnp.sum(returns * pushed_t[f : f + 1, :], axis=1, keepdims=True)
            gains = jnp.where(iota((8, BS), 1) == f, gain, gains)
        bmsg[:, 0:CELLS] = base
        bmsg[:, CELLS : CELLS + BS] = gains
        bin_[:, 0:CELLS] = base
        bin_[:, CELLS : CELLS + BS] = gains
        to_atmos.start()

    for i in range(RUN):

        @pl.when(jnp.logical_or(ocean, j != i))
        def _(i=i):
            remote(fx.at[i], fin.at[i], f_send.at[0, i], f_recv.at[i], at(1 - grp, z, i, s)).wait_recv()

    for c in range(RUN):
        ft[c * 4 : (c + 1) * 4, :] = fin[c, 0:4, :]
    ftab[s] = ft[...]

    def over_sub(source_of, table, leg):
        return [
            remote(
                source_of(sub_peers[d]),
                table.at[s],
                x_send.at[leg, d],
                x_recv.at[leg, d],
                at(grp, z, j, sub_peers[d]),
            )
            for d in range(1, n_sub)
        ]

    gather_copies = over_sub(lambda peer: ft, ftab, 0)
    for copy in gather_copies:
        copy.start()
    for copy in gather_copies:
        copy.wait_recv()

    n_rows = n_sub * ROWS
    high, low = pieces(ftab[...].reshape(n_rows, BS))
    table = jnp.concatenate([high, low], axis=1)
    row_owner = iota((n_rows, CELLS), 0) // 4
    ocean_flux = jnp.zeros((8, CELLS), F32)
    for k in range(3):
        taken = fast_dot(table, oh[:, k * CELLS : (k + 1) * CELLS], NN)
        taken = jnp.where(row_owner == owner[k : k + 1, :], taken, 0.0)
        taken = taken.reshape(n_rows // 8, 8, CELLS).sum(axis=0)
        ocean_flux = ocean_flux + rw[k : k + 1, :] * taken
    ocean_flux = ocean_flux + pltpu.roll(ocean_flux, 4, 0)

    @pl.when(atmos)
    def _():
        to_atmos.wait_recv()

    wet_f = wet[...].astype(F32)
    surface = bin_[:, 0:CELLS]
    for f in range(4):
        gain = bin_[:, CELLS + f : CELLS + f + 1]
        surface = surface + gain * ocean_flux[f : f + 1, :]
    surface = surface * wet_f
    surface = surface + pltpu.roll(surface, 4, 0)
    sums = None
    for k in range(3):
        high, low = pieces(surface * rw[k : k + 1, :])
        mine = row_owner == owner[k : k + 1, :]
        spread_out = []
        for piece in (high, low):
            tall = jnp.broadcast_to(piece.astype(F32)[None], (n_rows // 8, 8, CELLS))
            spread_out.append(jnp.where(mine, tall.reshape(n_rows, CELLS), 0.0).astype(BF16))
        part = fast_dot(
            jnp.concatenate(spread_out, axis=0), oh[0:BS, k * CELLS : (k + 1) * CELLS], NT
        )
        part = part[0:n_rows] + part[n_rows : 2 * n_rows]
        sums = part if sums is None else sums + part
    pbuf[...] = sums.reshape(n_sub, ROWS, BS)
    sum_copies = over_sub(lambda peer: pbuf.at[peer], cin, 1)
    for copy in sum_copies:
        copy.start()
    cin[s] = pbuf[s]

    @pl.when(atmos)
    def _():
        for copy in back_copies:
            copy.wait_recv()
        for r in range(RUN):
            nsb[:, r * BS : (r + 1) * BS] = jnp.transpose(rt[r])

    @pl.when(ocean)
    def _():
        columns = jnp.transpose(jnp.concatenate([pushed_t, jnp.zeros((BS - 8, BS), F32)], axis=0))
        for r in range(RUN):
            part = slice(r * BS, (r + 1) * BS)
            forced = jnp.transpose(rt[r])
            for f in range(4):
                forced = forced + columns[:, f : f + 1] * ocean_flux[f : f + 1, part]
            old = start[:, part]
            nsb[:, part] = old + wet_f[:, part] * (forced - old)

    out_state = pltpu.make_async_copy(nsb, ns_out.at[0], o_sem.at[0])
    out_state.start()

    for copy in sum_copies:
        copy.wait_recv()
    summed = cin[...].sum(axis=0)
    by_chunk = [rows8(summed[c * 4 : (c + 1) * 4, :]) for c in range(RUN)]
    for r, block in enumerate(regroup(by_chunk, RUN)):
        cplb[:, r * BS : (r + 1) * BS] = block[0:3, :]
    out_coupled = pltpu.make_async_copy(cplb, cpl_out, o_sem.at[1])
    out_coupled.start()

    for copy in index_copies + state_copies + back_copies + gather_copies + sum_copies:
        copy.wait_send()

    @pl.when(atmos)
    def _():
        for i, copy in enumerate(flux_copies(0)):

            @pl.when(j != i)
            def _(copy=copy):
                copy.wait_send()

        for copy in flux_copies(1):
            copy.wait_send()

    @pl.when(ocean)
    def _():
        to_atmos.wait_send()

    out_state.wait()
    out_coupled.wait()


def local(
    column_state,
    neighbours,
    mixing,
    diffusivity,
    flux_map,
    force_map,
    return_map,
    sources,
    remap_weights,
    wet,
):
    n_zone = lax.axis_size("reg") // RUN
    n_sub = lax.axis_size("sub")
    vmem, dma = pltpu.VMEM, pltpu.SemaphoreType.DMA
    i32 = jnp.int32
    scratch = [
        vmem((LEV, CELLS), F32),
        vmem((3, 1, CELLS), i32),
        vmem((LEV, LEV), F32),
        vmem((1, LEV), F32),
        vmem((4, LEV), F32),
        vmem((4, LEV), F32),
        vmem((3, LEV), F32),
        vmem((3, CELLS), i32),
        vmem((3, CELLS), F32),
        vmem((1, CELLS), i32),
        vmem((RUN, BS, LEV), F32),
        vmem((RUN, 8, BS), i32),
        vmem((RUN, 8, BS), i32),
        vmem((CELLS, SLOTS), BF16),
        vmem((STEPS + 1, 24, COLS, LEV), F32),
        vmem((STEPS, 2, 4, 8, LEV), F32),
        vmem((CELLS, LEV), F32),
        vmem((2 * LEV, 2 * LEV), BF16),
        vmem((2 * BS, 3 * CELLS), BF16),
        vmem((RUN, 8, BS), F32),
        vmem((RUN, 8, BS), F32),
        vmem((ROWS, BS), F32),
        vmem((n_sub, ROWS, BS), F32),
        vmem((RUN, BS, LEV), F32),
        vmem((8, CELLS + BS), F32),
        vmem((8, CELLS + BS), F32),
        vmem((n_sub, ROWS, BS), F32),
        vmem((n_sub, ROWS, BS), F32),
        vmem((LEV, CELLS), F32),
        vmem((3, CELLS), F32),
        dma((10,)),
        dma((2, RUN)),
        dma((2, RUN)),
        dma((STEPS, 16)),
        dma((STEPS, 16)),
        dma((2, RUN)),
        dma((RUN,)),
        dma((RUN,)),
        dma((RUN,)),
        dma((2, n_sub)),
        dma((2, n_sub)),
        dma(()),
        dma(()),
        dma((2,)),
    ]

    def kernel(*refs):
        body(n_zone, n_sub, *refs)

    anywhere = pl.BlockSpec(memory_space=pl.ANY)
    return pl.pallas_call(
        kernel,
        name="window",
        out_shape=(
            jax.ShapeDtypeStruct((1, LEV, CELLS), F32),
            jax.ShapeDtypeStruct((3, CELLS), F32),
        ),
        in_specs=[anywhere] * 10,
        out_specs=(anywhere, anywhere),
        scratch_shapes=scratch,
        compiler_params=pltpu.CompilerParams(
            collective_id=0, has_side_effects=True, vmem_limit_bytes=40 << 20
        ),
    )(
        column_state,
        neighbours.transpose(1, 0, 2),
        mixing,
        diffusivity,
        flux_map,
        force_map.T,
        return_map,
        sources,
        remap_weights,
        wet.reshape(1, CELLS),
    )


def solution(mesh):
    in_specs = (
        P("grp", None, ("reg", "sub")),
        P("grp", None, ("reg", "sub")),
        P("grp", None, None),
        P("grp", None),
        P(),
        P(),
        P(),
        P(None, ("reg", "sub")),
        P(None, ("reg", "sub")),
        P(("reg", "sub")),
    )
    out_specs = (P("grp", None, ("reg", "sub")), P(None, ("reg", "sub")))
    return jax.shard_map(local, mesh=mesh, in_specs=in_specs, out_specs=out_specs, check_vma=False)
```

```python
import jax
import jax.numpy as jnp
from jax import lax
from jax.experimental import pallas as pl
from jax.experimental.pallas import tpu as pltpu
from jax.sharding import PartitionSpec as P

LA = 90
LEV = 128
CELLS = 512
BS = 128
STEPS = 4
RUN = 4
COLS = 32
ROWS = 16
RIM = 8
EROWS = ROWS + 2 * RIM
ECOLS = COLS + 2 * RIM
BLOCK = 4 * ECOLS
BAND = 8 * ECOLS
TAG = 96
EXT = BS + 4
MESH = pl.DeviceIdType.MESH
F32 = jnp.float32
BF16 = jnp.bfloat16


def exact_dot(a, b, dims):
    return lax.dot_general(
        a, b, (dims, ((), ())), precision=lax.Precision.HIGHEST, preferred_element_type=F32
    )


def fast_dot(a, b, dims):
    return lax.dot_general(a, b, (dims, ((), ())), preferred_element_type=F32)


NN = ((1,), (0,))
NT = ((1,), (1,))


def pieces(x):
    high = x.astype(BF16)
    return high, (x - high.astype(F32)).astype(BF16)


def rows8(x):
    return jnp.concatenate([x, jnp.zeros((8 - x.shape[0], x.shape[1]), x.dtype)], axis=0)


def iota(shape, dim):
    return lax.broadcasted_iota(jnp.int32, shape, dim)


def lane_roll(x, shift):
    shift = shift % x.shape[1]
    return x if shift == 0 else pltpu.roll(x, shift, 1)


def regroup(parts, n):
    width = parts[0].shape[1] // n
    group = iota(parts[0].shape, 1) // width
    out = []
    for b in range(n):
        total = lane_roll(parts[0], -b * width)
        for a in range(1, n):
            total = jnp.where(group == a, lane_roll(parts[a], (a - b) * width), total)
        out.append(total)
    return out


def body(
    n_zone,
    n_sub,
    cs_in,
    nb_in,
    mix_in,
    rate_in,
    fm_in,
    force_in,
    rm_in,
    src_in,
    rw_in,
    wet_in,
    ns_out,
    cpl_out,
    start,
    nb,
    mixing,
    rate,
    fm,
    force,
    rm,
    src,
    rw,
    wet,
    vt,
    idq,
    nidx,
    lk,
    cnt,
    vx,
    sp,
    w2,
    oh,
    fx,
    fin,
    ft,
    ftab,
    rt,
    bmsg,
    bin_,
    pbuf,
    cin,
    in_sem,
    t_send,
    t_recv,
    h_send,
    h_recv,
    f_send,
    f_recv,
    r_send,
    r_recv,
    x_send,
    x_recv,
    b_send,
    b_recv,
):
    grp = lax.axis_index("grp")
    reg = lax.axis_index("reg")
    s = lax.axis_index("sub")
    z = reg // RUN
    j = reg % RUN
    odd = s % 2
    ocean = grp == 1
    atmos = grp == 0

    def chunk_of(place):
        return jnp.where(odd == 1, RUN - 1 - place, place)

    q = chunk_of(j)
    z_up = lax.rem(z + n_zone - 1, n_zone)
    z_down = lax.rem(z + 1, n_zone)
    s_before = lax.rem(s + n_sub - 1, n_sub)
    s_after = lax.rem(s + 1, n_sub)
    l_j = jnp.where(q == 0, j, chunk_of(q - 1))
    l_s = jnp.where(q == 0, s_before, s)
    r_j = jnp.where(q == RUN - 1, j, chunk_of(q + 1))
    r_s = jnp.where(q == RUN - 1, s_after, s)

    def at(g, zone, place, sub):
        return (g, zone * RUN + place, sub)

    run_peers = [j, j + 1 - 2 * (j % 2), lax.rem(j + 2, RUN), RUN - 1 - j]
    sub_peers = [lax.rem(s + d, n_sub) for d in range(n_sub)]
    halo_peers = [
        at(grp, z_up, j, s),
        at(grp, z_down, j, s),
        at(grp, z, l_j, l_s),
        at(grp, z, r_j, r_s),
        at(grp, z_up, l_j, l_s),
        at(grp, z_up, r_j, r_s),
        at(grp, z_down, l_j, l_s),
        at(grp, z_down, r_j, r_s),
    ]

    barrier = pltpu.get_barrier_semaphore()
    greeted = [at(grp, z, p, s) for p in run_peers[1:]]
    greeted += [at(1 - grp, z, p, s) for p in run_peers]
    greeted += [at(grp, z, j, p) for p in sub_peers[1:]]
    greeted += halo_peers
    for device in greeted:
        pl.semaphore_signal(barrier, inc=1, device_id=device, device_id_type=MESH)

    loads = [
        pltpu.make_async_copy(a, b, in_sem.at[n])
        for n, (a, b) in enumerate(
            [
                (cs_in.at[0], start),
                (nb_in, nb),
                (mix_in.at[0], mixing),
                (rate_in, rate),
                (fm_in, fm),
                (force_in, force),
                (rm_in, rm),
                (src_in, src),
                (rw_in, rw),
                (wet_in, wet),
            ]
        )
    ]
    for load in loads:
        load.start()

    lane = iota((1, LEV), 1)
    keep = jnp.logical_or(lane < LA, ocean).astype(F32)
    tagged = jnp.logical_and(lane >= TAG, lane < TAG + 3)
    carried = jnp.logical_or(jnp.logical_or(lane < LA, ocean), tagged).astype(F32)

    loads[1].wait()
    link = rows8(jnp.concatenate([nb[k] for k in range(3)], axis=0))
    e_row = jnp.zeros_like(link)
    for a in range(1, 8):
        e_row = e_row + (link >= a * EXT).astype(jnp.int32)
    cell = iota((8, CELLS), 1)
    offset = ECOLS * (e_row - 2 - cell // BS) + (link - e_row * EXT - 2 - cell % BS)
    offset = offset.astype(F32)
    blocks = regroup([offset[:, r * BS : (r + 1) * BS] for r in range(RUN)], RUN)
    for c, block in enumerate(blocks):
        idq[c] = block

    loads[0].wait()
    tags = jnp.concatenate([offset, jnp.zeros((LEV - TAG - 8, CELLS), F32)], axis=0)
    for r in range(RUN):
        part = slice(r * BS, (r + 1) * BS)
        tall = jnp.where(ocean, start[TAG:LEV, part], tags[:, part])
        tall = jnp.concatenate([start[0:TAG, part], tall], axis=0)
        vt[r] = jnp.transpose(tall) * carried

    pl.semaphore_wait(barrier, len(greeted))

    def remote(source, target, send, recv, device):
        return pltpu.make_async_remote_copy(
            src_ref=source,
            dst_ref=target,
            send_sem=send,
            recv_sem=recv,
            device_id=device,
            device_id_type=MESH,
        )

    index_copies, state_copies = [], []
    for d in range(1, RUN):
        peer = run_peers[d]
        c = chunk_of(peer)
        index_copies.append(
            remote(idq.at[c], nidx.at[j], t_send.at[0, d], t_recv.at[0, d], at(grp, z, peer, s))
        )
        state_copies.append(
            remote(
                vt.at[:, pl.ds(pl.multiple_of(c * COLS, COLS), COLS), :],
                vx.at[0, pl.ds(RIM + j * RUN, RUN), pl.ds(RIM, COLS)],
                t_send.at[1, d],
                t_recv.at[1, d],
                at(grp, z, peer, s),
            )
        )

    @pl.when(ocean)
    def _():
        for copy in index_copies:
            copy.start()

    for copy in state_copies:
        copy.start()
    nidx[j] = idq[q]
    for r in range(RUN):
        piece = vt[r, pl.ds(pl.multiple_of(q * COLS, COLS), COLS), :]
        vx[0, RIM + j * RUN + r, RIM : RIM + COLS, :] = piece

    def halo_copies(i):
        rows = pl.ds(RIM + RUN * i, RUN)
        up = i < 2
        zone = jnp.where(up, z_up, z_down)
        landing = pl.ds(jnp.where(up, EROWS - RIM + RUN * i, RUN * i - RIM), RUN)
        inner, first, end = pl.ds(RIM, COLS), pl.ds(RIM, RIM), pl.ds(COLS, RIM)
        before, after = pl.ds(0, RIM), pl.ds(RIM + COLS, RIM)
        here = vx.at[0]
        routes = [
            (here.at[rows, inner], here.at[landing, inner], at(grp, zone, j, s)),
            (here.at[rows, first], here.at[landing, after], at(grp, zone, l_j, l_s)),
            (here.at[rows, end], here.at[landing, before], at(grp, zone, r_j, r_s)),
            (here.at[rows, first], here.at[rows, after], at(grp, z, l_j, l_s)),
            (here.at[rows, end], here.at[rows, before], at(grp, z, r_j, r_s)),
        ]
        return [
            remote(source, target, h_send.at[kind, i], h_recv.at[kind, i], device)
            for kind, (source, target, device) in enumerate(routes)
        ]

    for copy in halo_copies(j):
        copy.start()

    loads[2].wait()
    used = jnp.logical_or(iota((LEV, LEV), 0) < LA, ocean)
    m_high, m_low = pieces(jnp.where(used, jnp.transpose(mixing[...]), 0.0))
    for a in range(2):
        w2[a * LEV : (a + 1) * LEV, 0:LEV] = m_high
        w2[a * LEV : (a + 1) * LEV, LEV : 2 * LEV] = m_low

    loads[7].wait()
    place = src[...]
    owner = (place // CELLS) * RUN + (place % BS) // COLS
    inside = ((place % CELLS) // BS) * COLS + place % COLS
    for k in range(3):
        hot = (iota((BS, CELLS), 0) == inside[k : k + 1, :]).astype(F32).astype(BF16)
        oh[0:BS, k * CELLS : (k + 1) * CELLS] = hot
        oh[BS : 2 * BS, k * CELLS : (k + 1) * CELLS] = hot

    for slot, first in ((1, 0), (1, EROWS - 2), (3, 4), (3, EROWS - 6)):
        spot = slice(first * ECOLS, (first + 2) * ECOLS)
        sp[slot, spot, :] = jnp.zeros((2 * ECOLS, 2 * LEV), BF16)

    loads[3].wait()
    for d in range(1, RUN):
        state_copies[d - 1].wait_recv()
        for copy in halo_copies(run_peers[d]):
            copy.start()

    gap = iota((BLOCK, BAND), 1) - iota((BLOCK, BAND), 0) - 2 * ECOLS
    gap = gap.astype(F32)

    def count(b, offsets, first):
        total = (offsets[:, first : first + 1] == gap).astype(F32)
        for k in range(1, 3):
            total = total + (offsets[:, first + k : first + k + 1] == gap).astype(F32)
        cnt[b] = total.astype(BF16)

    @pl.when(ocean)
    def _():
        for copy in index_copies:
            copy.wait_recv()
        lk[...] = jnp.zeros_like(lk)
        for i in range(RUN):
            tall = jnp.concatenate([nidx[i], jnp.zeros((BS - 8, BS), F32)], axis=0)
            tall = jnp.transpose(tall)
            for r in range(RUN):
                lk[RIM + RUN * i + r, RIM : RIM + COLS, :] = tall[r * COLS : (r + 1) * COLS]

        def one(b, carry):
            count(b, lk[pl.ds(4 * b + 2, 4)].reshape(BLOCK, LEV), 0)
            return carry

        lax.fori_loop(0, 7, one, 0)

    for i in range(RUN):
        for copy in halo_copies(i):
            copy.wait_recv()

    @pl.when(atmos)
    def _():
        def one(b, carry):
            count(b, vx[0, pl.ds(4 * b + 2, 4)].reshape(BLOCK, LEV), TAG)
            return carry

        lax.fori_loop(0, 7, one, 0)

    for row in range(0, EROWS, 4):
        high, low = pieces(vx[0, row : row + 4].reshape(BLOCK, LEV))
        sp[0, row * ECOLS : (row + 4) * ECOLS, 0:LEV] = high
        sp[0, row * ECOLS : (row + 4) * ECOLS, LEV : 2 * LEV] = low

    def step(n, blocks):
        for b in blocks:
            row = 4 * b + 2
            acc = fast_dot(cnt[b], sp[n, 4 * b * ECOLS : 4 * b * ECOLS + BAND, :], NN)
            field = vx[n, row : row + 4].reshape(BLOCK, LEV)
            total = acc[:, 0:LEV] + acc[:, LEV : 2 * LEV]
            spread = field + rate[...] * (total - 3.0 * field)
            high, low = pieces(spread)
            mixed = fast_dot(jnp.concatenate([high, low], axis=1), w2[...], NN)
            new = keep * (spread + mixed[:, 0:LEV] + mixed[:, LEV : 2 * LEV])
            vx[n + 1, row : row + 4] = new.reshape(4, ECOLS, LEV)
            high, low = pieces(new)
            sp[n + 1, row * ECOLS : row * ECOLS + BLOCK, 0:LEV] = high
            sp[n + 1, row * ECOLS : row * ECOLS + BLOCK, LEV : 2 * LEV] = low

    def wide(n, carry):
        step(n, range(7))
        return carry

    def narrow(n, carry):
        step(n, range(1, 6))
        return carry

    n_steps = jnp.where(ocean, 1, STEPS)
    lax.fori_loop(0, jnp.where(ocean, 1, 2), wide, 0)
    lax.fori_loop(jnp.where(ocean, STEPS, 2), STEPS, narrow, 0)

    def own(n):
        return vx[n, RIM : RIM + ROWS, RIM : RIM + COLS, :].reshape(CELLS, LEV)

    def flux_copies(g):
        return [
            remote(
                fx.at[i],
                fin.at[q],
                f_send.at[g, i],
                f_recv.at[j],
                at(g, z, i, s),
            )
            for i in range(RUN)
        ]

    loads[4].wait()

    @pl.when(atmos)
    def _():
        flux = exact_dot(rows8(fm[...]), own(1) + own(2) + own(3) + own(4), NT) * (1.0 / STEPS)
        for i in range(RUN):
            fx[i] = flux[:, i * BS : (i + 1) * BS]
        for i, copy in enumerate(flux_copies(0)):

            @pl.when(j != i)
            def _(copy=copy):
                copy.start()

        for copy in flux_copies(1):
            copy.start()
        fin[q] = fx[j]

    last = n_steps
    back_copies = []
    for d in range(1, RUN):
        peer = run_peers[d]
        back_copies.append(
            remote(
                vx.at[last, pl.ds(RIM + peer * RUN, RUN), pl.ds(RIM, COLS)],
                rt.at[:, pl.ds(pl.multiple_of(q * COLS, COLS), COLS), :],
                r_send.at[d],
                r_recv.at[d],
                at(grp, z, peer, s),
            )
        )

    @pl.when(ocean)
    def _():
        for copy in back_copies:
            copy.start()

    for r in range(RUN):
        piece = vx[last, RIM + j * RUN + r, RIM : RIM + COLS, :]
        rt[r, pl.ds(pl.multiple_of(q * COLS, COLS), COLS), :] = piece

    loads[5].wait()
    loads[6].wait()
    loads[8].wait()
    loads[9].wait()
    to_atmos = remote(bmsg, bin_, b_send, b_recv, at(1 - grp, z, j, s))
    force_t = rows8(force[...])
    pushed_t = force_t + exact_dot(force_t, mixing[...], NT)

    @pl.when(ocean)
    def _():
        for copy in back_copies:
            copy.wait_recv()
        returns = rows8(rm[...])
        base = exact_dot(returns, rt[...].reshape(CELLS, LEV), NT)
        gains = jnp.zeros((8, BS), F32)
        for f in range(4):
            gain = jnp.sum(returns * pushed_t[f : f + 1, :], axis=1, keepdims=True)
            gains = jnp.where(iota((8, BS), 1) == f, gain, gains)
        bmsg[:, 0:CELLS] = base
        bmsg[:, CELLS : CELLS + BS] = gains
        bin_[:, 0:CELLS] = base
        bin_[:, CELLS : CELLS + BS] = gains
        to_atmos.start()

    for i in range(RUN):

        @pl.when(jnp.logical_or(ocean, j != i))
        def _(i=i):
            remote(fx.at[i], fin.at[i], f_send.at[0, i], f_recv.at[i], at(1 - grp, z, i, s)).wait_recv()

    for c in range(RUN):
        ft[c * 4 : (c + 1) * 4, :] = fin[c, 0:4, :]
    ftab[s] = ft[...]

    def over_sub(source_of, table, leg):
        return [
            remote(
                source_of(sub_peers[d]),
                table.at[s],
                x_send.at[leg, d],
                x_recv.at[leg, d],
                at(grp, z, j, sub_peers[d]),
            )
            for d in range(1, n_sub)
        ]

    gather_copies = over_sub(lambda peer: ft, ftab, 0)
    for copy in gather_copies:
        copy.start()

    @pl.when(atmos)
    def _():
        for copy in back_copies:
            copy.start()

    for copy in gather_copies:
        copy.wait_recv()

    n_rows = n_sub * ROWS
    high, low = pieces(ftab[...].reshape(n_rows, BS))
    table = jnp.concatenate([high, low], axis=1)
    row_owner = iota((n_rows, CELLS), 0) // 4
    ocean_flux = jnp.zeros((8, CELLS), F32)
    for k in range(3):
        taken = fast_dot(table, oh[:, k * CELLS : (k + 1) * CELLS], NN)
        taken = jnp.where(row_owner == owner[k : k + 1, :], taken, 0.0)
        taken = taken.reshape(n_rows // 8, 8, CELLS).sum(axis=0)
        ocean_flux = ocean_flux + rw[k : k + 1, :] * taken
    ocean_flux = ocean_flux + pltpu.roll(ocean_flux, 4, 0)

    @pl.when(atmos)
    def _():
        to_atmos.wait_recv()

    wet_f = wet[...].astype(F32)
    surface = bin_[:, 0:CELLS]
    for f in range(4):
        gain = bin_[:, CELLS + f : CELLS + f + 1]
        surface = surface + gain * ocean_flux[f : f + 1, :]
    surface = surface * wet_f
    surface = surface + pltpu.roll(surface, 4, 0)
    sums = None
    for k in range(3):
        high, low = pieces(surface * rw[k : k + 1, :])
        mine = row_owner == owner[k : k + 1, :]
        spread_out = []
        for piece in (high, low):
            tall = jnp.broadcast_to(piece.astype(F32)[None], (n_rows // 8, 8, CELLS))
            spread_out.append(jnp.where(mine, tall.reshape(n_rows, CELLS), 0.0).astype(BF16))
        part = fast_dot(
            jnp.concatenate(spread_out, axis=0), oh[0:BS, k * CELLS : (k + 1) * CELLS], NT
        )
        part = part[0:n_rows] + part[n_rows : 2 * n_rows]
        sums = part if sums is None else sums + part
    pbuf[...] = sums.reshape(n_sub, ROWS, BS)
    sum_copies = over_sub(lambda peer: pbuf.at[peer], cin, 1)
    for copy in sum_copies:
        copy.start()
    cin[s] = pbuf[s]

    @pl.when(atmos)
    def _():
        for copy in back_copies:
            copy.wait_recv()
        for r in range(RUN):
            ns_out[0, :, r * BS : (r + 1) * BS] = jnp.transpose(rt[r])

    @pl.when(ocean)
    def _():
        columns = jnp.transpose(jnp.concatenate([pushed_t, jnp.zeros((BS - 8, BS), F32)], axis=0))
        for r in range(RUN):
            part = slice(r * BS, (r + 1) * BS)
            forced = jnp.transpose(rt[r])
            for f in range(4):
                forced = forced + columns[:, f : f + 1] * ocean_flux[f : f + 1, part]
            old = start[:, part]
            ns_out[0, :, part] = old + wet_f[:, part] * (forced - old)

    for copy in sum_copies:
        copy.wait_recv()
    summed = cin[...].sum(axis=0)
    by_chunk = [rows8(summed[c * 4 : (c + 1) * 4, :]) for c in range(RUN)]
    for r, block in enumerate(regroup(by_chunk, RUN)):
        cpl_out[:, r * BS : (r + 1) * BS] = block[0:3, :]

    for copy in state_copies + back_copies + gather_copies + sum_copies:
        copy.wait_send()
    for i in range(RUN):
        for copy in halo_copies(i):
            copy.wait_send()

    @pl.when(atmos)
    def _():
        for i, copy in enumerate(flux_copies(0)):

            @pl.when(j != i)
            def _(copy=copy):
                copy.wait_send()

        for copy in flux_copies(1):
            copy.wait_send()

    @pl.when(ocean)
    def _():
        to_atmos.wait_send()
        for copy in index_copies:
            copy.wait_send()


def local(
    column_state,
    neighbours,
    mixing,
    diffusivity,
    flux_map,
    force_map,
    return_map,
    sources,
    remap_weights,
    wet,
):
    n_zone = lax.axis_size("reg") // RUN
    n_sub = lax.axis_size("sub")
    vmem, dma = pltpu.VMEM, pltpu.SemaphoreType.DMA
    i32 = jnp.int32
    scratch = [
        vmem((LEV, CELLS), F32),
        vmem((3, 1, CELLS), i32),
        vmem((LEV, LEV), F32),
        vmem((1, LEV), F32),
        vmem((4, LEV), F32),
        vmem((4, LEV), F32),
        vmem((3, LEV), F32),
        vmem((3, CELLS), i32),
        vmem((3, CELLS), F32),
        vmem((1, CELLS), i32),
        vmem((RUN, BS, LEV), F32),
        vmem((RUN, 8, BS), F32),
        vmem((RUN, 8, BS), F32),
        vmem((EROWS, ECOLS, LEV), F32),
        vmem((7, BLOCK, BAND), BF16),
        vmem((STEPS + 1, EROWS, ECOLS, LEV), F32),
        vmem((STEPS + 1, EROWS * ECOLS, 2 * LEV), BF16),
        vmem((2 * LEV, 2 * LEV), BF16),
        vmem((2 * BS, 3 * CELLS), BF16),
        vmem((RUN, 8, BS), F32),
        vmem((RUN, 8, BS), F32),
        vmem((ROWS, BS), F32),
        vmem((n_sub, ROWS, BS), F32),
        vmem((RUN, BS, LEV), F32),
        vmem((8, CELLS + BS), F32),
        vmem((8, CELLS + BS), F32),
        vmem((n_sub, ROWS, BS), F32),
        vmem((n_sub, ROWS, BS), F32),
        dma((10,)),
        dma((2, RUN)),
        dma((2, RUN)),
        dma((5, RUN)),
        dma((5, RUN)),
        dma((2, RUN)),
        dma((RUN,)),
        dma((RUN,)),
        dma((RUN,)),
        dma((2, n_sub)),
        dma((2, n_sub)),
        dma(()),
        dma(()),
    ]

    def kernel(*refs):
        body(n_zone, n_sub, *refs)

    return pl.pallas_call(
        kernel,
        name="window",
        out_shape=(
            jax.ShapeDtypeStruct((1, LEV, CELLS), F32),
            jax.ShapeDtypeStruct((3, CELLS), F32),
        ),
        in_specs=[pl.BlockSpec(memory_space=pltpu.HBM)] * 10,
        out_specs=(pl.BlockSpec(memory_space=pltpu.VMEM),) * 2,
        scratch_shapes=scratch,
        compiler_params=pltpu.CompilerParams(
            collective_id=0, has_side_effects=True, vmem_limit_bytes=40 << 20
        ),
    )(*[pltpu.with_memory_space_constraint(a, pltpu.HBM) for a in (
        column_state,
        neighbours.transpose(1, 0, 2),
        mixing,
        diffusivity,
        flux_map,
        force_map.T,
        return_map,
        sources,
        remap_weights,
        wet.reshape(1, CELLS),
    )])


def solution(mesh):
    in_specs = (
        P("grp", None, ("reg", "sub")),
        P("grp", None, ("reg", "sub")),
        P("grp", None, None),
        P("grp", None),
        P(),
        P(),
        P(),
        P(None, ("reg", "sub")),
        P(None, ("reg", "sub")),
        P(("reg", "sub")),
    )
    out_specs = (P("grp", None, ("reg", "sub")), P(None, ("reg", "sub")))
    return jax.shard_map(local, mesh=mesh, in_specs=in_specs, out_specs=out_specs, check_vma=False)
```

```python
import jax
import jax.numpy as jnp
from jax import lax
from jax.experimental import pallas as pl
from jax.experimental.pallas import tpu as pltpu
from jax.sharding import PartitionSpec as P

LA = 90
LEV = 128
CELLS = 512
BS = 128
STEPS = 4
RUN = 4
COLS = 32
ROWS = 16
RIM = 8
EROWS = ROWS + 2 * RIM
ECOLS = COLS + 2 * RIM
BLOCK = 4 * ECOLS
BAND = 8 * ECOLS
TAG = LA
PACK = 96
THIRD = PACK // 3
EXT = BS + 4
MESH = pl.DeviceIdType.MESH
F32 = jnp.float32
BF16 = jnp.bfloat16


def exact_dot(a, b, dims):
    return lax.dot_general(
        a, b, (dims, ((), ())), precision=lax.Precision.HIGHEST, preferred_element_type=F32
    )


def fast_dot(a, b, dims):
    return lax.dot_general(a, b, (dims, ((), ())), preferred_element_type=F32)


NN = ((1,), (0,))
NT = ((1,), (1,))


def pieces(x):
    high = x.astype(BF16)
    return high, (x - high.astype(F32)).astype(BF16)


def rows8(x):
    return jnp.concatenate([x, jnp.zeros((8 - x.shape[0], x.shape[1]), x.dtype)], axis=0)


def iota(shape, dim):
    return lax.broadcasted_iota(jnp.int32, shape, dim)


def lane_roll(x, shift):
    shift = shift % x.shape[1]
    return x if shift == 0 else pltpu.roll(x, shift, 1)


def regroup(parts, n):
    width = parts[0].shape[1] // n
    group = iota(parts[0].shape, 1) // width
    out = []
    for b in range(n):
        total = lane_roll(parts[0], -b * width)
        for a in range(1, n):
            total = jnp.where(group == a, lane_roll(parts[a], (a - b) * width), total)
        out.append(total)
    return out


def body(
    n_zone,
    n_sub,
    cs_in,
    nb_in,
    mix_in,
    rate_in,
    fm_in,
    force_in,
    rm_in,
    src_in,
    rw_in,
    wet_in,
    ns_out,
    cpl_out,
    start,
    nb,
    mixing,
    rate,
    fm,
    force,
    rm,
    src,
    rw,
    wet,
    vt,
    idq,
    nidx,
    lk,
    cnt,
    vx,
    sp,
    w2,
    oh,
    fx,
    fin,
    ft,
    ftab,
    rt,
    bmsg,
    bin_,
    pbuf,
    cin,
    in_sem,
    t_send,
    t_recv,
    h_send,
    h_recv,
    f_send,
    f_recv,
    r_send,
    r_recv,
    x_send,
    x_recv,
    b_send,
    b_recv,
):
    grp = lax.axis_index("grp")
    reg = lax.axis_index("reg")
    s = lax.axis_index("sub")
    z = reg // RUN
    j = reg % RUN
    odd = s % 2
    ocean = grp == 1
    atmos = grp == 0

    def chunk_of(place):
        return jnp.where(odd == 1, RUN - 1 - place, place)

    q = chunk_of(j)
    z_up = lax.rem(z + n_zone - 1, n_zone)
    z_down = lax.rem(z + 1, n_zone)
    s_before = lax.rem(s + n_sub - 1, n_sub)
    s_after = lax.rem(s + 1, n_sub)
    l_j = jnp.where(q == 0, j, chunk_of(q - 1))
    l_s = jnp.where(q == 0, s_before, s)
    r_j = jnp.where(q == RUN - 1, j, chunk_of(q + 1))
    r_s = jnp.where(q == RUN - 1, s_after, s)

    def at(g, zone, place, sub):
        return (g, zone * RUN + place, sub)

    run_peers = [j, j + 1 - 2 * (j % 2), lax.rem(j + 2, RUN), RUN - 1 - j]
    sub_peers = [lax.rem(s + d, n_sub) for d in range(n_sub)]
    halo_peers = [
        at(grp, z_up, j, s),
        at(grp, z_down, j, s),
        at(grp, z, l_j, l_s),
        at(grp, z, r_j, r_s),
        at(grp, z_up, l_j, l_s),
        at(grp, z_up, r_j, r_s),
        at(grp, z_down, l_j, l_s),
        at(grp, z_down, r_j, r_s),
    ]

    barrier = pltpu.get_barrier_semaphore()
    greeted = [at(grp, z, p, s) for p in run_peers[1:]]
    greeted += [at(1 - grp, z, p, s) for p in run_peers]
    greeted += [at(grp, z, j, p) for p in sub_peers[1:]]
    greeted += halo_peers
    for device in greeted:
        pl.semaphore_signal(barrier, inc=1, device_id=device, device_id_type=MESH)

    loads = [
        pltpu.make_async_copy(a, b, in_sem.at[n])
        for n, (a, b) in enumerate(
            [
                (nb_in, nb),
                (mix_in.at[0], mixing),
                (rate_in, rate),
                (fm_in, fm),
                (force_in, force),
                (rm_in, rm),
                (src_in, src),
                (rw_in, rw),
                (wet_in, wet),
            ]
        )
    ]
    columns = [
        pltpu.make_async_copy(
            cs_in.at[0, :, pl.ds(r * BS, BS)], start.at[:, pl.ds(r * BS, BS)], in_sem.at[9 + r]
        )
        for r in range(RUN)
    ]
    loads[0].start()
    for r in (3, 0, 1, 2):
        columns[r].start()
    for load in loads[1:]:
        load.start()

    lane = iota((1, LEV), 1)
    keep = jnp.logical_or(lane < LA, ocean).astype(F32)
    loads[0].wait()
    link = rows8(jnp.concatenate([nb[k] for k in range(3)], axis=0))
    e_row = jnp.zeros_like(link)
    for a in range(1, 8):
        e_row = e_row + (link >= a * EXT).astype(jnp.int32)
    cell = iota((8, CELLS), 1)
    offset = ECOLS * (e_row - 2 - cell // BS) + (link - e_row * EXT - 2 - cell % BS)
    offset = offset.astype(F32)

    @pl.when(ocean)
    def _():
        blocks = regroup([offset[:, r * BS : (r + 1) * BS] for r in range(RUN)], RUN)
        for c, block in enumerate(blocks):
            idq[c] = block
        for r in range(RUN):
            columns[r].wait()
            vt[r] = jnp.transpose(start[:, r * BS : (r + 1) * BS])

    @pl.when(atmos)
    def _():
        at_tag = TAG % 8
        row = iota((8, BS), 0)
        tags = pltpu.roll(offset, at_tag, 0)
        packed = None
        for r in (3, 0, 1, 2):
            columns[r].wait()
            part = slice(r * BS, (r + 1) * BS)
            mixed_rows = jnp.where(row < at_tag + 3, tags[:, part], 0.0)
            mixed_rows = jnp.where(row < at_tag, start[TAG - at_tag : PACK, part], mixed_rows)
            tall = [start[0 : TAG - at_tag, part], mixed_rows, jnp.zeros((LEV - PACK, BS), F32)]
            tall = jnp.transpose(jnp.concatenate(tall, axis=0))
            if packed is None:
                packed = tall
            else:
                tall = jnp.where(lane < PACK, tall, lane_roll(packed, PACK - r * THIRD))
            vt[r] = tall

    pl.semaphore_wait(barrier, len(greeted))

    def remote(source, target, send, recv, device):
        return pltpu.make_async_remote_copy(
            src_ref=source,
            dst_ref=target,
            send_sem=send,
            recv_sem=recv,
            device_id=device,
            device_id_type=MESH,
        )

    index_copies, state_copies, rest_copies = [], [], []
    for d in range(1, RUN):
        peer = run_peers[d]
        c = chunk_of(peer)
        there = at(grp, z, peer, s)
        index_copies.append(
            remote(idq.at[c], nidx.at[j], t_send.at[0, d], t_recv.at[0, d], there)
        )
        cells = pl.ds(pl.multiple_of(c * COLS, COLS), COLS)
        for part, copies, first, count in ((1, state_copies, 0, 3), (2, rest_copies, 3, 1)):
            copies.append(
                remote(
                    vt.at[pl.ds(first, count), cells, :],
                    vx.at[0, pl.ds(RIM + j * RUN + first, count), pl.ds(RIM, COLS)],
                    t_send.at[part, d],
                    t_recv.at[part, d],
                    there,
                )
            )

    for copy in state_copies:
        copy.start()

    @pl.when(ocean)
    def _():
        for copy in rest_copies + index_copies:
            copy.start()
        nidx[j] = idq[q]

    for r in range(RUN):
        piece = vt[r, pl.ds(pl.multiple_of(q * COLS, COLS), COLS), :]
        vx[0, RIM + j * RUN + r, RIM : RIM + COLS, :] = piece

    def halo_copies(i, rest=0, kinds=range(5)):
        first_row = RUN * i + (3 if rest else 0)
        rows = pl.ds(RIM + first_row, 1 if rest else 3)
        up = i < 2
        zone = jnp.where(up, z_up, z_down)
        landing = jnp.where(up, EROWS - RIM + first_row, first_row - RIM)
        landing = pl.ds(landing, 1 if rest else 3)
        inner, first, end = pl.ds(RIM, COLS), pl.ds(RIM, RIM), pl.ds(COLS, RIM)
        before, after = pl.ds(0, RIM), pl.ds(RIM + COLS, RIM)
        here = vx.at[0]
        routes = [
            (here.at[rows, inner], here.at[landing, inner], at(grp, zone, j, s)),
            (here.at[rows, first], here.at[landing, after], at(grp, zone, l_j, l_s)),
            (here.at[rows, end], here.at[landing, before], at(grp, zone, r_j, r_s)),
            (here.at[rows, first], here.at[rows, after], at(grp, z, l_j, l_s)),
            (here.at[rows, end], here.at[rows, before], at(grp, z, r_j, r_s)),
        ]
        return [
            remote(source, target, h_send.at[rest, kind, i], h_recv.at[rest, kind, i], device)
            for kind, (source, target, device) in enumerate(routes)
            if kind in kinds
        ]

    def send_halo(i):
        for copy in halo_copies(i):
            copy.start()

        @pl.when(ocean)
        def _():
            for copy in halo_copies(i, 1):
                copy.start()

    def await_halo(i, kinds):
        for copy in halo_copies(i, 0, kinds):
            copy.wait_recv()

        @pl.when(ocean)
        def _():
            for copy in halo_copies(i, 1, kinds):
                copy.wait_recv()

    send_halo(j)

    loads[1].wait()
    used = jnp.logical_or(iota((LEV, LEV), 0) < LA, ocean)
    m_high, m_low = pieces(jnp.where(used, jnp.transpose(mixing[...]), 0.0))
    for a in range(2):
        w2[a * LEV : (a + 1) * LEV, 0:LEV] = m_high
        w2[a * LEV : (a + 1) * LEV, LEV : 2 * LEV] = m_low

    loads[6].wait()
    place = src[...]
    owner = (place // CELLS) * RUN + (place % BS) // COLS
    inside = ((place % CELLS) // BS) * COLS + place % COLS
    for k in range(3):
        hot = (iota((BS, CELLS), 0) == inside[k : k + 1, :]).astype(F32).astype(BF16)
        oh[0:BS, k * CELLS : (k + 1) * CELLS] = hot
        oh[BS : 2 * BS, k * CELLS : (k + 1) * CELLS] = hot

    for slot, first in ((1, 0), (1, EROWS - 2), (3, 4), (3, EROWS - 6)):
        spot = slice(first * ECOLS, (first + 2) * ECOLS)
        sp[slot, spot, :] = jnp.zeros((2 * ECOLS, 2 * LEV), BF16)

    loads[2].wait()
    for d in range(1, RUN):
        state_copies[d - 1].wait_recv()

        @pl.when(ocean)
        def _(d=d):
            rest_copies[d - 1].wait_recv()

        send_halo(run_peers[d])

    gap = iota((BLOCK, BAND), 1) - iota((BLOCK, BAND), 0) - 2 * ECOLS
    gap = gap.astype(F32)

    def count(b, offsets, first):
        total = (offsets[:, first : first + 1] == gap).astype(F32)
        for k in range(1, 3):
            total = total + (offsets[:, first + k : first + k + 1] == gap).astype(F32)
        cnt[b] = total.astype(BF16)

    @pl.when(ocean)
    def _():
        for copy in index_copies:
            copy.wait_recv()
        lk[...] = jnp.zeros_like(lk)
        for i in range(RUN):
            tall = jnp.concatenate([nidx[i], jnp.zeros((BS - 8, BS), F32)], axis=0)
            tall = jnp.transpose(tall)
            for r in range(RUN):
                lk[RIM + RUN * i + r, RIM : RIM + COLS, :] = tall[r * COLS : (r + 1) * COLS]

        def one(b, carry):
            count(b, lk[pl.ds(4 * b + 2, 4)].reshape(BLOCK, LEV), 0)
            return carry

        lax.fori_loop(0, 7, one, 0)

    def count_blocks(first, end):
        @pl.when(atmos)
        def _():
            def one(b, carry):
                count(b, vx[0, pl.ds(4 * b + 2, 4)].reshape(BLOCK, LEV), TAG)
                return carry

            lax.fori_loop(first, end, one, 0)

    def unpack(first, end):
        @pl.when(atmos)
        def _():
            for g in range(first, end):
                fourth = lane_roll(vx[0, 4 * g], THIRD)
                for r in range(1, 3):
                    moved = lane_roll(vx[0, 4 * g + r], (r + 1) * THIRD + LEV - PACK - THIRD)
                    fourth = jnp.where(lane < r * THIRD, fourth, moved)
                vx[0, 4 * g + 3] = fourth

        for g in range(first, end):
            high, low = pieces(vx[0, 4 * g : 4 * g + 4].reshape(BLOCK, LEV))
            sp[0, 4 * g * ECOLS : (4 * g + 4) * ECOLS, 0:LEV] = high
            sp[0, 4 * g * ECOLS : (4 * g + 4) * ECOLS, LEV : 2 * LEV] = low

    for i in range(RUN):
        await_halo(i, (3, 4))
    unpack(2, 6)
    count_blocks(2, 5)
    for i in (2, 3):
        await_halo(i, (0, 1, 2))
    unpack(0, 2)
    count_blocks(0, 2)
    for i in (0, 1):
        await_halo(i, (0, 1, 2))
    unpack(6, 8)
    count_blocks(5, 7)

    def step(n, blocks):
        for b in blocks:
            row = 4 * b + 2
            acc = fast_dot(cnt[b], sp[n, 4 * b * ECOLS : 4 * b * ECOLS + BAND, :], NN)
            field = vx[n, row : row + 4].reshape(BLOCK, LEV)
            total = acc[:, 0:LEV] + acc[:, LEV : 2 * LEV]
            spread = field + rate[...] * (total - 3.0 * field)
            high, low = pieces(spread)
            mixed = fast_dot(jnp.concatenate([high, low], axis=1), w2[...], NN)
            new = keep * (spread + mixed[:, 0:LEV] + mixed[:, LEV : 2 * LEV])
            vx[n + 1, row : row + 4] = new.reshape(4, ECOLS, LEV)
            high, low = pieces(new)
            sp[n + 1, row * ECOLS : row * ECOLS + BLOCK, 0:LEV] = high
            sp[n + 1, row * ECOLS : row * ECOLS + BLOCK, LEV : 2 * LEV] = low

    def wide(n, carry):
        step(n, range(7))
        return carry

    def narrow(n, carry):
        step(n, range(1, 6))
        return carry

    n_steps = jnp.where(ocean, 1, STEPS)
    lax.fori_loop(0, jnp.where(ocean, 1, 2), wide, 0)
    lax.fori_loop(jnp.where(ocean, STEPS, 2), STEPS, narrow, 0)

    def own(n):
        return vx[n, RIM : RIM + ROWS, RIM : RIM + COLS, :].reshape(CELLS, LEV)

    def flux_copies(g):
        return [
            remote(
                fx.at[i],
                fin.at[q],
                f_send.at[g, i],
                f_recv.at[j],
                at(g, z, i, s),
            )
            for i in range(RUN)
        ]

    loads[3].wait()

    @pl.when(atmos)
    def _():
        f_high, f_low = pieces(rows8(fm[...]) * (1.0 / STEPS))
        v_high, v_low = pieces(own(1) + own(2) + own(3) + own(4))
        weights = jnp.concatenate([f_high, f_low], axis=0)
        flux = fast_dot(weights, v_high, NT)
        flux = flux[0:8] + flux[8:16] + fast_dot(f_high, v_low, NT)
        for i in range(RUN):
            fx[i] = flux[:, i * BS : (i + 1) * BS]
        for i, copy in enumerate(flux_copies(0)):

            @pl.when(j != i)
            def _(copy=copy):
                copy.start()

        for copy in flux_copies(1):
            copy.start()
        fin[q] = fx[j]

    last = n_steps
    back_copies = []
    for d in range(1, RUN):
        peer = run_peers[d]
        back_copies.append(
            remote(
                vx.at[last, pl.ds(RIM + peer * RUN, RUN), pl.ds(RIM, COLS)],
                rt.at[:, pl.ds(pl.multiple_of(q * COLS, COLS), COLS), :],
                r_send.at[d],
                r_recv.at[d],
                at(grp, z, peer, s),
            )
        )

    @pl.when(ocean)
    def _():
        for copy in back_copies:
            copy.start()

    for r in range(RUN):
        piece = vx[last, RIM + j * RUN + r, RIM : RIM + COLS, :]
        rt[r, pl.ds(pl.multiple_of(q * COLS, COLS), COLS), :] = piece

    loads[4].wait()
    loads[5].wait()
    loads[7].wait()
    loads[8].wait()
    to_atmos = remote(bmsg, bin_, b_send, b_recv, at(1 - grp, z, j, s))
    force_t = rows8(force[...])
    pushed_t = force_t + exact_dot(force_t, mixing[...], NT)

    @pl.when(ocean)
    def _():
        for copy in back_copies:
            copy.wait_recv()
        returns = rows8(rm[...])
        base = exact_dot(returns, rt[...].reshape(CELLS, LEV), NT)
        gains = jnp.zeros((8, BS), F32)
        for f in range(4):
            gain = jnp.sum(returns * pushed_t[f : f + 1, :], axis=1, keepdims=True)
            gains = jnp.where(iota((8, BS), 1) == f, gain, gains)
        bmsg[:, 0:CELLS] = base
        bmsg[:, CELLS : CELLS + BS] = gains
        bin_[:, 0:CELLS] = base
        bin_[:, CELLS : CELLS + BS] = gains
        to_atmos.start()

    for i in range(RUN):

        @pl.when(jnp.logical_or(ocean, j != i))
        def _(i=i):
            remote(fx.at[i], fin.at[i], f_send.at[0, i], f_recv.at[i], at(1 - grp, z, i, s)).wait_recv()

    for c in range(RUN):
        ft[c * 4 : (c + 1) * 4, :] = fin[c, 0:4, :]
    ftab[s] = ft[...]

    def over_sub(source_of, table, leg):
        return [
            remote(
                source_of(sub_peers[d]),
                table.at[s],
                x_send.at[leg, d],
                x_recv.at[leg, d],
                at(grp, z, j, sub_peers[d]),
            )
            for d in range(1, n_sub)
        ]

    gather_copies = over_sub(lambda peer: ft, ftab, 0)
    for copy in gather_copies:
        copy.start()

    @pl.when(atmos)
    def _():
        for copy in back_copies:
            copy.start()

    for copy in gather_copies:
        copy.wait_recv()

    n_rows = n_sub * ROWS
    high, low = pieces(ftab[...].reshape(n_rows, BS))
    table = jnp.concatenate([high, low], axis=1)
    row_owner = iota((n_rows, CELLS), 0) // 4
    ocean_flux = jnp.zeros((8, CELLS), F32)
    for k in range(3):
        taken = fast_dot(table, oh[:, k * CELLS : (k + 1) * CELLS], NN)
        taken = jnp.where(row_owner == owner[k : k + 1, :], taken, 0.0)
        taken = taken.reshape(n_rows // 8, 8, CELLS).sum(axis=0)
        ocean_flux = ocean_flux + rw[k : k + 1, :] * taken
    ocean_flux = ocean_flux + pltpu.roll(ocean_flux, 4, 0)

    @pl.when(atmos)
    def _():
        to_atmos.wait_recv()

    wet_f = wet[...].astype(F32)
    surface = bin_[:, 0:CELLS]
    for f in range(4):
        gain = bin_[:, CELLS + f : CELLS + f + 1]
        surface = surface + gain * ocean_flux[f : f + 1, :]
    surface = surface * wet_f
    surface = surface + pltpu.roll(surface, 4, 0)
    sums = None
    for k in range(3):
        high, low = pieces(surface * rw[k : k + 1, :])
        mine = row_owner == owner[k : k + 1, :]
        spread_out = []
        for piece in (high, low):
            tall = jnp.broadcast_to(piece.astype(F32)[None], (n_rows // 8, 8, CELLS))
            spread_out.append(jnp.where(mine, tall.reshape(n_rows, CELLS), 0.0).astype(BF16))
        part = fast_dot(
            jnp.concatenate(spread_out, axis=0), oh[0:BS, k * CELLS : (k + 1) * CELLS], NT
        )
        part = part[0:n_rows] + part[n_rows : 2 * n_rows]
        sums = part if sums is None else sums + part
    pbuf[...] = sums.reshape(n_sub, ROWS, BS)
    sum_copies = over_sub(lambda peer: pbuf.at[peer], cin, 1)
    for copy in sum_copies:
        copy.start()
    cin[s] = pbuf[s]

    @pl.when(atmos)
    def _():
        for copy in back_copies:
            copy.wait_recv()
        for r in range(RUN):
            ns_out[0, :, r * BS : (r + 1) * BS] = jnp.transpose(rt[r])

    @pl.when(ocean)
    def _():
        columns = jnp.transpose(jnp.concatenate([pushed_t, jnp.zeros((BS - 8, BS), F32)], axis=0))
        for r in range(RUN):
            part = slice(r * BS, (r + 1) * BS)
            forced = jnp.transpose(rt[r])
            for f in range(4):
                forced = forced + columns[:, f : f + 1] * ocean_flux[f : f + 1, part]
            old = start[:, part]
            ns_out[0, :, part] = old + wet_f[:, part] * (forced - old)

    for copy in sum_copies:
        copy.wait_recv()
    summed = cin[...].sum(axis=0)
    by_chunk = [rows8(summed[c * 4 : (c + 1) * 4, :]) for c in range(RUN)]
    for r, block in enumerate(regroup(by_chunk, RUN)):
        cpl_out[:, r * BS : (r + 1) * BS] = block[0:3, :]

    for copy in state_copies + back_copies + gather_copies + sum_copies:
        copy.wait_send()
    for i in range(RUN):
        for copy in halo_copies(i):
            copy.wait_send()

        @pl.when(ocean)
        def _(i=i):
            for copy in halo_copies(i, 1):
                copy.wait_send()


    @pl.when(atmos)
    def _():
        for i, copy in enumerate(flux_copies(0)):

            @pl.when(j != i)
            def _(copy=copy):
                copy.wait_send()

        for copy in flux_copies(1):
            copy.wait_send()

    @pl.when(ocean)
    def _():
        to_atmos.wait_send()
        for copy in index_copies + rest_copies:
            copy.wait_send()


def local(
    column_state,
    neighbours,
    mixing,
    diffusivity,
    flux_map,
    force_map,
    return_map,
    sources,
    remap_weights,
    wet,
):
    n_zone = lax.axis_size("reg") // RUN
    n_sub = lax.axis_size("sub")
    vmem, dma = pltpu.VMEM, pltpu.SemaphoreType.DMA
    i32 = jnp.int32
    scratch = [
        vmem((LEV, CELLS), F32),
        vmem((3, 1, CELLS), i32),
        vmem((LEV, LEV), F32),
        vmem((1, LEV), F32),
        vmem((4, LEV), F32),
        vmem((4, LEV), F32),
        vmem((3, LEV), F32),
        vmem((3, CELLS), i32),
        vmem((3, CELLS), F32),
        vmem((1, CELLS), i32),
        vmem((RUN, BS, LEV), F32),
        vmem((RUN, 8, BS), F32),
        vmem((RUN, 8, BS), F32),
        vmem((EROWS, ECOLS, LEV), F32),
        vmem((7, BLOCK, BAND), BF16),
        vmem((STEPS + 1, EROWS, ECOLS, LEV), F32),
        vmem((STEPS + 1, EROWS * ECOLS, 2 * LEV), BF16),
        vmem((2 * LEV, 2 * LEV), BF16),
        vmem((2 * BS, 3 * CELLS), BF16),
        vmem((RUN, 8, BS), F32),
        vmem((RUN, 8, BS), F32),
        vmem((ROWS, BS), F32),
        vmem((n_sub, ROWS, BS), F32),
        vmem((RUN, BS, LEV), F32),
        vmem((8, CELLS + BS), F32),
        vmem((8, CELLS + BS), F32),
        vmem((n_sub, ROWS, BS), F32),
        vmem((n_sub, ROWS, BS), F32),
        dma((9 + RUN,)),
        dma((3, RUN)),
        dma((3, RUN)),
        dma((2, 5, RUN)),
        dma((2, 5, RUN)),
        dma((2, RUN)),
        dma((RUN,)),
        dma((RUN,)),
        dma((RUN,)),
        dma((2, n_sub)),
        dma((2, n_sub)),
        dma(()),
        dma(()),
    ]

    def kernel(*refs):
        body(n_zone, n_sub, *refs)

    return pl.pallas_call(
        kernel,
        name="window",
        out_shape=(
            jax.ShapeDtypeStruct((1, LEV, CELLS), F32),
            jax.ShapeDtypeStruct((3, CELLS), F32),
        ),
        in_specs=[pl.BlockSpec(memory_space=pltpu.HBM)] * 10,
        out_specs=(pl.BlockSpec(memory_space=pltpu.VMEM),) * 2,
        scratch_shapes=scratch,
        compiler_params=pltpu.CompilerParams(
            collective_id=0, has_side_effects=True, vmem_limit_bytes=40 << 20
        ),
    )(*[pltpu.with_memory_space_constraint(a, pltpu.HBM) for a in (
        column_state,
        neighbours.transpose(1, 0, 2),
        mixing,
        diffusivity,
        flux_map,
        force_map.T,
        return_map,
        sources,
        remap_weights,
        wet.reshape(1, CELLS),
    )])


def solution(mesh):
    in_specs = (
        P("grp", None, ("reg", "sub")),
        P("grp", None, ("reg", "sub")),
        P("grp", None, None),
        P("grp", None),
        P(),
        P(),
        P(),
        P(None, ("reg", "sub")),
        P(None, ("reg", "sub")),
        P(("reg", "sub")),
    )
    out_specs = (P("grp", None, ("reg", "sub")), P(None, ("reg", "sub")))
    return jax.shard_map(local, mesh=mesh, in_specs=in_specs, out_specs=out_specs, check_vma=False)
```

```python
import jax
import jax.numpy as jnp
from jax import lax
from jax.experimental import pallas as pl
from jax.experimental.pallas import tpu as pltpu
from jax.sharding import PartitionSpec as P

LA = 90
LEV = 128
CELLS = 512
BS = 128
STEPS = 4
RUN = 4
COLS = 32
ROWS = 16
RIM = 8
EROWS = ROWS + 2 * RIM
ECOLS = COLS + 2 * RIM
BLOCK = 4 * ECOLS
BAND = 8 * ECOLS
TAG = LA
PACK = 96
THIRD = PACK // 3
EXT = BS + 4
MESH = pl.DeviceIdType.MESH
F32 = jnp.float32
BF16 = jnp.bfloat16


def exact_dot(a, b, dims):
    return lax.dot_general(
        a, b, (dims, ((), ())), precision=lax.Precision.HIGHEST, preferred_element_type=F32
    )


def fast_dot(a, b, dims):
    return lax.dot_general(a, b, (dims, ((), ())), preferred_element_type=F32)


NN = ((1,), (0,))
NT = ((1,), (1,))


def pieces(x):
    high = x.astype(BF16)
    return high, (x - high.astype(F32)).astype(BF16)


def rows8(x):
    return jnp.concatenate([x, jnp.zeros((8 - x.shape[0], x.shape[1]), x.dtype)], axis=0)


def iota(shape, dim):
    return lax.broadcasted_iota(jnp.int32, shape, dim)


def lane_roll(x, shift):
    shift = shift % x.shape[1]
    return x if shift == 0 else pltpu.roll(x, shift, 1)


def regroup(parts, n):
    width = parts[0].shape[1] // n
    group = iota(parts[0].shape, 1) // width
    out = []
    for b in range(n):
        total = lane_roll(parts[0], -b * width)
        for a in range(1, n):
            total = jnp.where(group == a, lane_roll(parts[a], (a - b) * width), total)
        out.append(total)
    return out


def body(
    n_zone,
    n_sub,
    cs_in,
    nb_in,
    mix_in,
    rate_in,
    fm_in,
    force_in,
    rm_in,
    src_in,
    rw_in,
    wet_in,
    ns_out,
    cpl_out,
    start,
    nb,
    mixing,
    rate,
    fm,
    force,
    rm,
    src,
    rw,
    wet,
    vt,
    idq,
    nidx,
    lk,
    cnt,
    vx,
    sp,
    w2,
    oh,
    fx,
    fin,
    ft,
    ftab,
    rt,
    bx,
    bin_,
    gx,
    gin,
    pbuf,
    cin,
    in_sem,
    t_send,
    t_recv,
    h_send,
    h_recv,
    f_send,
    f_recv,
    r_send,
    r_recv,
    x_send,
    x_recv,
    b_send,
    b_recv,
    g_send,
    g_recv,
):
    grp = lax.axis_index("grp")
    reg = lax.axis_index("reg")
    s = lax.axis_index("sub")
    z = reg // RUN
    j = reg % RUN
    odd = s % 2
    ocean = grp == 1
    atmos = grp == 0

    def chunk_of(place):
        return jnp.where(odd == 1, RUN - 1 - place, place)

    q = chunk_of(j)
    z_up = lax.rem(z + n_zone - 1, n_zone)
    z_down = lax.rem(z + 1, n_zone)
    s_before = lax.rem(s + n_sub - 1, n_sub)
    s_after = lax.rem(s + 1, n_sub)
    l_j = jnp.where(q == 0, j, chunk_of(q - 1))
    l_s = jnp.where(q == 0, s_before, s)
    r_j = jnp.where(q == RUN - 1, j, chunk_of(q + 1))
    r_s = jnp.where(q == RUN - 1, s_after, s)

    def at(g, zone, place, sub):
        return (g, zone * RUN + place, sub)

    run_peers = [j, j + 1 - 2 * (j % 2), lax.rem(j + 2, RUN), RUN - 1 - j]
    sub_peers = [lax.rem(s + d, n_sub) for d in range(n_sub)]
    halo_peers = [
        at(grp, z_up, j, s),
        at(grp, z_down, j, s),
        at(grp, z, l_j, l_s),
        at(grp, z, r_j, r_s),
        at(grp, z_up, l_j, l_s),
        at(grp, z_up, r_j, r_s),
        at(grp, z_down, l_j, l_s),
        at(grp, z_down, r_j, r_s),
    ]

    barrier = pltpu.get_barrier_semaphore()
    greeted = [at(grp, z, p, s) for p in run_peers[1:]]
    greeted += [at(1 - grp, z, p, s) for p in run_peers]
    greeted += [at(grp, z, j, p) for p in sub_peers[1:]]
    greeted += halo_peers
    for device in greeted:
        pl.semaphore_signal(barrier, inc=1, device_id=device, device_id_type=MESH)

    loads = [
        pltpu.make_async_copy(a, b, in_sem.at[n])
        for n, (a, b) in enumerate(
            [
                (nb_in, nb),
                (mix_in.at[0], mixing),
                (rate_in, rate),
                (fm_in, fm),
                (force_in, force),
                (rm_in, rm),
                (src_in, src),
                (rw_in, rw),
                (wet_in, wet),
            ]
        )
    ]
    columns = [
        pltpu.make_async_copy(
            cs_in.at[0, :, pl.ds(r * BS, BS)], start.at[:, pl.ds(r * BS, BS)], in_sem.at[9 + r]
        )
        for r in range(RUN)
    ]
    loads[0].start()
    for r in (3, 0, 1, 2):
        columns[r].start()
    for load in loads[1:]:
        load.start()

    lane = iota((1, LEV), 1)
    keep = jnp.logical_or(lane < LA, ocean).astype(F32)
    loads[0].wait()
    link = rows8(jnp.concatenate([nb[k] for k in range(3)], axis=0))
    e_row = jnp.zeros_like(link)
    for a in range(1, 8):
        e_row = e_row + (link >= a * EXT).astype(jnp.int32)
    cell = iota((8, CELLS), 1)
    offset = ECOLS * (e_row - 2 - cell // BS) + (link - e_row * EXT - 2 - cell % BS)
    offset = offset.astype(F32)

    @pl.when(ocean)
    def _():
        blocks = regroup([offset[:, r * BS : (r + 1) * BS] for r in range(RUN)], RUN)
        for c, block in enumerate(blocks):
            idq[c] = block
        for r in range(RUN):
            columns[r].wait()
            vt[r] = jnp.transpose(start[:, r * BS : (r + 1) * BS])

    @pl.when(atmos)
    def _():
        at_tag = TAG % 8
        row = iota((8, BS), 0)
        tags = pltpu.roll(offset, at_tag, 0)
        packed = None
        for r in (3, 0, 1, 2):
            columns[r].wait()
            part = slice(r * BS, (r + 1) * BS)
            mixed_rows = jnp.where(row < at_tag + 3, tags[:, part], 0.0)
            mixed_rows = jnp.where(row < at_tag, start[TAG - at_tag : PACK, part], mixed_rows)
            tall = [start[0 : TAG - at_tag, part], mixed_rows, jnp.zeros((LEV - PACK, BS), F32)]
            tall = jnp.transpose(jnp.concatenate(tall, axis=0))
            if packed is None:
                packed = tall
            else:
                tall = jnp.where(lane < PACK, tall, lane_roll(packed, PACK - r * THIRD))
            vt[r] = tall

    pl.semaphore_wait(barrier, len(greeted))

    def remote(source, target, send, recv, device):
        return pltpu.make_async_remote_copy(
            src_ref=source,
            dst_ref=target,
            send_sem=send,
            recv_sem=recv,
            device_id=device,
            device_id_type=MESH,
        )

    index_copies, state_copies, rest_copies = [], [], []
    for d in range(1, RUN):
        peer = run_peers[d]
        c = chunk_of(peer)
        there = at(grp, z, peer, s)
        index_copies.append(
            remote(idq.at[c], nidx.at[j], t_send.at[0, d], t_recv.at[0, d], there)
        )
        cells = pl.ds(pl.multiple_of(c * COLS, COLS), COLS)
        for part, copies, first, count in ((1, state_copies, 0, 3), (2, rest_copies, 3, 1)):
            copies.append(
                remote(
                    vt.at[pl.ds(first, count), cells, :],
                    vx.at[0, pl.ds(RIM + j * RUN + first, count), pl.ds(RIM, COLS)],
                    t_send.at[part, d],
                    t_recv.at[part, d],
                    there,
                )
            )

    for copy in state_copies:
        copy.start()

    @pl.when(ocean)
    def _():
        for copy in rest_copies + index_copies:
            copy.start()
        nidx[j] = idq[q]

    for r in range(RUN):
        piece = vt[r, pl.ds(pl.multiple_of(q * COLS, COLS), COLS), :]
        vx[0, RIM + j * RUN + r, RIM : RIM + COLS, :] = piece

    def halo_copies(i, rest=0, kinds=range(5)):
        first_row = RUN * i + (3 if rest else 0)
        rows = pl.ds(RIM + first_row, 1 if rest else 3)
        up = i < 2
        zone = jnp.where(up, z_up, z_down)
        landing = jnp.where(up, EROWS - RIM + first_row, first_row - RIM)
        landing = pl.ds(landing, 1 if rest else 3)
        inner, first, end = pl.ds(RIM, COLS), pl.ds(RIM, RIM), pl.ds(COLS, RIM)
        before, after = pl.ds(0, RIM), pl.ds(RIM + COLS, RIM)
        here = vx.at[0]
        routes = [
            (here.at[rows, inner], here.at[landing, inner], at(grp, zone, j, s)),
            (here.at[rows, first], here.at[landing, after], at(grp, zone, l_j, l_s)),
            (here.at[rows, end], here.at[landing, before], at(grp, zone, r_j, r_s)),
            (here.at[rows, first], here.at[rows, after], at(grp, z, l_j, l_s)),
            (here.at[rows, end], here.at[rows, before], at(grp, z, r_j, r_s)),
        ]
        return [
            remote(source, target, h_send.at[rest, kind, i], h_recv.at[rest, kind, i], device)
            for kind, (source, target, device) in enumerate(routes)
            if kind in kinds
        ]

    def send_halo(i):
        for copy in halo_copies(i):
            copy.start()

        @pl.when(ocean)
        def _():
            for copy in halo_copies(i, 1):
                copy.start()

    def await_halo(i, kinds):
        for copy in halo_copies(i, 0, kinds):
            copy.wait_recv()

        @pl.when(ocean)
        def _():
            for copy in halo_copies(i, 1, kinds):
                copy.wait_recv()

    send_halo(j)

    loads[1].wait()
    used = jnp.logical_or(iota((LEV, LEV), 0) < LA, ocean)
    m_high, m_low = pieces(jnp.where(used, jnp.transpose(mixing[...]), 0.0))
    for a in range(2):
        w2[a * LEV : (a + 1) * LEV, 0:LEV] = m_high
        w2[a * LEV : (a + 1) * LEV, LEV : 2 * LEV] = m_low

    loads[6].wait()
    place = src[...]
    owner = (place // CELLS) * RUN + (place % BS) // COLS
    inside = ((place % CELLS) // BS) * COLS + place % COLS
    for k in range(3):
        hot = (iota((BS, CELLS), 0) == inside[k : k + 1, :]).astype(F32).astype(BF16)
        oh[0:BS, k * CELLS : (k + 1) * CELLS] = hot
        oh[BS : 2 * BS, k * CELLS : (k + 1) * CELLS] = hot

    for slot, first in ((1, 0), (1, EROWS - 2), (3, 4), (3, EROWS - 6)):
        spot = slice(first * ECOLS, (first + 2) * ECOLS)
        sp[slot, spot, :] = jnp.zeros((2 * ECOLS, 2 * LEV), BF16)

    loads[2].wait()
    for d in range(1, RUN):
        state_copies[d - 1].wait_recv()

        @pl.when(ocean)
        def _(d=d):
            rest_copies[d - 1].wait_recv()

        send_halo(run_peers[d])

    gap = iota((BLOCK, BAND), 1) - iota((BLOCK, BAND), 0) - 2 * ECOLS
    gap = gap.astype(F32)

    def count(b, offsets, first):
        total = (offsets[:, first : first + 1] == gap).astype(F32)
        for k in range(1, 3):
            total = total + (offsets[:, first + k : first + k + 1] == gap).astype(F32)
        cnt[b] = total.astype(BF16)

    @pl.when(ocean)
    def _():
        for copy in index_copies:
            copy.wait_recv()
        lk[...] = jnp.zeros_like(lk)
        for i in range(RUN):
            tall = jnp.concatenate([nidx[i], jnp.zeros((BS - 8, BS), F32)], axis=0)
            tall = jnp.transpose(tall)
            for r in range(RUN):
                lk[RIM + RUN * i + r, RIM : RIM + COLS, :] = tall[r * COLS : (r + 1) * COLS]

        def one(b, carry):
            count(b, lk[pl.ds(4 * b + 2, 4)].reshape(BLOCK, LEV), 0)
            return carry

        lax.fori_loop(0, 7, one, 0)

    def count_blocks(first, end):
        @pl.when(atmos)
        def _():
            def one(b, carry):
                count(b, vx[0, pl.ds(4 * b + 2, 4)].reshape(BLOCK, LEV), TAG)
                return carry

            lax.fori_loop(first, end, one, 0)

    def unpack(first, end):
        @pl.when(atmos)
        def _():
            for g in range(first, end):
                fourth = lane_roll(vx[0, 4 * g], THIRD)
                for r in range(1, 3):
                    moved = lane_roll(vx[0, 4 * g + r], (r + 1) * THIRD + LEV - PACK - THIRD)
                    fourth = jnp.where(lane < r * THIRD, fourth, moved)
                vx[0, 4 * g + 3] = fourth

        for g in range(first, end):
            high, low = pieces(vx[0, 4 * g : 4 * g + 4].reshape(BLOCK, LEV))
            sp[0, 4 * g * ECOLS : (4 * g + 4) * ECOLS, 0:LEV] = high
            sp[0, 4 * g * ECOLS : (4 * g + 4) * ECOLS, LEV : 2 * LEV] = low

    for i in range(RUN):
        await_halo(i, (3, 4))
    unpack(2, 6)
    count_blocks(2, 5)
    for i in (2, 3):
        await_halo(i, (0, 1, 2))
    unpack(0, 2)
    count_blocks(0, 2)
    for i in (0, 1):
        await_halo(i, (0, 1, 2))
    unpack(6, 8)
    count_blocks(5, 7)

    def step(n, blocks):
        for b in blocks:
            row = 4 * b + 2
            acc = fast_dot(cnt[b], sp[n, 4 * b * ECOLS : 4 * b * ECOLS + BAND, :], NN)
            field = vx[n, row : row + 4].reshape(BLOCK, LEV)
            total = acc[:, 0:LEV] + acc[:, LEV : 2 * LEV]
            spread = field + rate[...] * (total - 3.0 * field)
            high, low = pieces(spread)
            mixed = fast_dot(jnp.concatenate([high, low], axis=1), w2[...], NN)
            new = keep * (spread + mixed[:, 0:LEV] + mixed[:, LEV : 2 * LEV])
            vx[n + 1, row : row + 4] = new.reshape(4, ECOLS, LEV)
            high, low = pieces(new)
            sp[n + 1, row * ECOLS : row * ECOLS + BLOCK, 0:LEV] = high
            sp[n + 1, row * ECOLS : row * ECOLS + BLOCK, LEV : 2 * LEV] = low

    def wide(n, carry):
        step(n, range(7))
        return carry

    def narrow(n, carry):
        step(n, range(1, 6))
        return carry

    n_steps = jnp.where(ocean, 1, STEPS)
    lax.fori_loop(0, jnp.where(ocean, 1, 2), wide, 0)
    lax.fori_loop(jnp.where(ocean, STEPS, 2), STEPS, narrow, 0)

    def own(n):
        return vx[n, RIM : RIM + ROWS, RIM : RIM + COLS, :].reshape(CELLS, LEV)

    def to_owners(g, source, target, send, recv):
        return [
            remote(source.at[i], target.at[q], send.at[g, i], recv.at[j], at(g, z, i, s))
            for i in range(RUN)
        ]

    def flux_copies(g):
        return to_owners(g, fx, fin, f_send, f_recv)

    def base_copies(g):
        return to_owners(g, bx, bin_, b_send, b_recv)

    def but_own(copies, act):
        for i, copy in enumerate(copies):

            @pl.when(j != i)
            def _(copy=copy):
                act(copy)

    loads[3].wait()

    @pl.when(atmos)
    def _():
        f_high, f_low = pieces(rows8(fm[...]) * (1.0 / STEPS))
        v_high, v_low = pieces(own(1) + own(2) + own(3) + own(4))
        weights = jnp.concatenate([f_high, f_low], axis=0)
        flux = fast_dot(weights, v_high, NT)
        flux = flux[0:8] + flux[8:16] + fast_dot(f_high, v_low, NT)
        for i in range(RUN):
            fx[i] = flux[:, i * BS : (i + 1) * BS]
        for copy in flux_copies(1):
            copy.start()
        but_own(flux_copies(0), lambda copy: copy.start())
        fin[q] = fx[j]

    last = n_steps
    back_copies = []
    for d in range(1, RUN):
        peer = run_peers[d]
        back_copies.append(
            remote(
                vx.at[last, pl.ds(RIM + peer * RUN, RUN), pl.ds(RIM, COLS)],
                rt.at[:, pl.ds(pl.multiple_of(q * COLS, COLS), COLS), :],
                r_send.at[d],
                r_recv.at[d],
                at(grp, z, peer, s),
            )
        )

    loads[4].wait()
    loads[5].wait()
    loads[7].wait()
    loads[8].wait()
    to_atmos = remote(gx, gin, g_send, g_recv, at(1 - grp, z, j, s))
    force_t = rows8(force[...])
    pushed_t = force_t + exact_dot(force_t, mixing[...], NT)

    @pl.when(ocean)
    def _():
        returns = rows8(rm[...])
        base = exact_dot(returns, own(1), NT)
        for i in range(RUN):
            bx[i] = base[:, i * BS : (i + 1) * BS]
        for copy in base_copies(0):
            copy.start()
        but_own(base_copies(1), lambda copy: copy.start())
        bin_[q] = bx[j]
        gains = jnp.zeros((8, BS), F32)
        for f in range(4):
            gain = jnp.sum(returns * pushed_t[f : f + 1, :], axis=1, keepdims=True)
            gains = jnp.where(iota((8, BS), 1) == f, gain, gains)
        gx[...] = gains
        gin[...] = gains
        to_atmos.start()

    for r in range(RUN):
        piece = vx[last, RIM + j * RUN + r, RIM : RIM + COLS, :]
        rt[r, pl.ds(pl.multiple_of(q * COLS, COLS), COLS), :] = piece

    for i in range(RUN):

        @pl.when(jnp.logical_or(ocean, j != i))
        def _(i=i):
            remote(fx.at[i], fin.at[i], f_send.at[0, i], f_recv.at[i], at(1 - grp, z, i, s)).wait_recv()

    for c in range(RUN):
        ft[c * 4 : (c + 1) * 4, :] = fin[c, 0:4, :]
    ftab[s] = ft[...]

    def over_sub(source_of, table, leg):
        return [
            remote(
                source_of(sub_peers[d]),
                table.at[s],
                x_send.at[leg, d],
                x_recv.at[leg, d],
                at(grp, z, j, sub_peers[d]),
            )
            for d in range(1, n_sub)
        ]

    gather_copies = over_sub(lambda peer: ft, ftab, 0)
    for copy in gather_copies:
        copy.start()

    for copy in back_copies:
        copy.start()

    for i in range(RUN):

        @pl.when(jnp.logical_or(atmos, j != i))
        def _(i=i):
            device = at(1 - grp, z, i, s)
            remote(bx.at[i], bin_.at[i], b_send.at[0, i], b_recv.at[i], device).wait_recv()

    @pl.when(atmos)
    def _():
        to_atmos.wait_recv()

    base = regroup([bin_[c] for c in range(RUN)], RUN)
    base = jnp.concatenate(base, axis=1)

    for copy in gather_copies:
        copy.wait_recv()

    n_rows = n_sub * ROWS
    high, low = pieces(ftab[...].reshape(n_rows, BS))
    table = jnp.concatenate([high, low], axis=1)
    row_owner = iota((n_rows, CELLS), 0) // 4
    ocean_flux = jnp.zeros((8, CELLS), F32)
    for k in range(3):
        taken = fast_dot(table, oh[:, k * CELLS : (k + 1) * CELLS], NN)
        taken = jnp.where(row_owner == owner[k : k + 1, :], taken, 0.0)
        taken = taken.reshape(n_rows // 8, 8, CELLS).sum(axis=0)
        ocean_flux = ocean_flux + rw[k : k + 1, :] * taken
    ocean_flux = ocean_flux + pltpu.roll(ocean_flux, 4, 0)

    wet_f = wet[...].astype(F32)
    surface = base
    for f in range(4):
        surface = surface + gin[:, f : f + 1] * ocean_flux[f : f + 1, :]
    surface = surface * wet_f
    surface = surface + pltpu.roll(surface, 4, 0)
    sums = None
    for k in range(3):
        high, low = pieces(surface * rw[k : k + 1, :])
        mine = row_owner == owner[k : k + 1, :]
        spread_out = []
        for piece in (high, low):
            tall = jnp.broadcast_to(piece.astype(F32)[None], (n_rows // 8, 8, CELLS))
            spread_out.append(jnp.where(mine, tall.reshape(n_rows, CELLS), 0.0).astype(BF16))
        part = fast_dot(
            jnp.concatenate(spread_out, axis=0), oh[0:BS, k * CELLS : (k + 1) * CELLS], NT
        )
        part = part[0:n_rows] + part[n_rows : 2 * n_rows]
        sums = part if sums is None else sums + part
    pbuf[...] = sums.reshape(n_sub, ROWS, BS)
    sum_copies = over_sub(lambda peer: pbuf.at[peer], cin, 1)
    for copy in sum_copies:
        copy.start()
    cin[s] = pbuf[s]

    for copy in back_copies:
        copy.wait_recv()

    @pl.when(atmos)
    def _():
        for r in range(RUN):
            ns_out[0, :, r * BS : (r + 1) * BS] = jnp.transpose(rt[r])

    @pl.when(ocean)
    def _():
        columns = jnp.transpose(jnp.concatenate([pushed_t, jnp.zeros((BS - 8, BS), F32)], axis=0))
        for r in range(RUN):
            part = slice(r * BS, (r + 1) * BS)
            forced = jnp.transpose(rt[r])
            for f in range(4):
                forced = forced + columns[:, f : f + 1] * ocean_flux[f : f + 1, part]
            old = start[:, part]
            ns_out[0, :, part] = old + wet_f[:, part] * (forced - old)

    for copy in sum_copies:
        copy.wait_recv()
    summed = cin[...].sum(axis=0)
    by_chunk = [rows8(summed[c * 4 : (c + 1) * 4, :]) for c in range(RUN)]
    for r, block in enumerate(regroup(by_chunk, RUN)):
        cpl_out[:, r * BS : (r + 1) * BS] = block[0:3, :]

    for copy in state_copies + back_copies + gather_copies + sum_copies:
        copy.wait_send()
    for i in range(RUN):
        for copy in halo_copies(i):
            copy.wait_send()

        @pl.when(ocean)
        def _(i=i):
            for copy in halo_copies(i, 1):
                copy.wait_send()


    @pl.when(atmos)
    def _():
        but_own(flux_copies(0), lambda copy: copy.wait_send())
        for copy in flux_copies(1):
            copy.wait_send()

    @pl.when(ocean)
    def _():
        to_atmos.wait_send()
        but_own(base_copies(1), lambda copy: copy.wait_send())
        for copy in base_copies(0):
            copy.wait_send()
        for copy in index_copies + rest_copies:
            copy.wait_send()


def local(
    column_state,
    neighbours,
    mixing,
    diffusivity,
    flux_map,
    force_map,
    return_map,
    sources,
    remap_weights,
    wet,
):
    n_zone = lax.axis_size("reg") // RUN
    n_sub = lax.axis_size("sub")
    vmem, dma = pltpu.VMEM, pltpu.SemaphoreType.DMA
    i32 = jnp.int32
    scratch = [
        vmem((LEV, CELLS), F32),
        vmem((3, 1, CELLS), i32),
        vmem((LEV, LEV), F32),
        vmem((1, LEV), F32),
        vmem((4, LEV), F32),
        vmem((4, LEV), F32),
        vmem((3, LEV), F32),
        vmem((3, CELLS), i32),
        vmem((3, CELLS), F32),
        vmem((1, CELLS), i32),
        vmem((RUN, BS, LEV), F32),
        vmem((RUN, 8, BS), F32),
        vmem((RUN, 8, BS), F32),
        vmem((EROWS, ECOLS, LEV), F32),
        vmem((7, BLOCK, BAND), BF16),
        vmem((STEPS + 1, EROWS, ECOLS, LEV), F32),
        vmem((STEPS + 1, EROWS * ECOLS, 2 * LEV), BF16),
        vmem((2 * LEV, 2 * LEV), BF16),
        vmem((2 * BS, 3 * CELLS), BF16),
        vmem((RUN, 8, BS), F32),
        vmem((RUN, 8, BS), F32),
        vmem((ROWS, BS), F32),
        vmem((n_sub, ROWS, BS), F32),
        vmem((RUN, BS, LEV), F32),
        vmem((RUN, 8, BS), F32),
        vmem((RUN, 8, BS), F32),
        vmem((8, BS), F32),
        vmem((8, BS), F32),
        vmem((n_sub, ROWS, BS), F32),
        vmem((n_sub, ROWS, BS), F32),
        dma((9 + RUN,)),
        dma((3, RUN)),
        dma((3, RUN)),
        dma((2, 5, RUN)),
        dma((2, 5, RUN)),
        dma((2, RUN)),
        dma((RUN,)),
        dma((RUN,)),
        dma((RUN,)),
        dma((2, n_sub)),
        dma((2, n_sub)),
        dma((2, RUN)),
        dma((RUN,)),
        dma(()),
        dma(()),
    ]

    def kernel(*refs):
        body(n_zone, n_sub, *refs)

    return pl.pallas_call(
        kernel,
        name="window",
        out_shape=(
            jax.ShapeDtypeStruct((1, LEV, CELLS), F32),
            jax.ShapeDtypeStruct((3, CELLS), F32),
        ),
        in_specs=[pl.BlockSpec(memory_space=pltpu.HBM)] * 10,
        out_specs=(pl.BlockSpec(memory_space=pltpu.VMEM),) * 2,
        scratch_shapes=scratch,
        compiler_params=pltpu.CompilerParams(
            collective_id=0, has_side_effects=True, vmem_limit_bytes=40 << 20
        ),
    )(*[pltpu.with_memory_space_constraint(a, pltpu.HBM) for a in (
        column_state,
        neighbours.transpose(1, 0, 2),
        mixing,
        diffusivity,
        flux_map,
        force_map.T,
        return_map,
        sources,
        remap_weights,
        wet.reshape(1, CELLS),
    )])


def solution(mesh):
    in_specs = (
        P("grp", None, ("reg", "sub")),
        P("grp", None, ("reg", "sub")),
        P("grp", None, None),
        P("grp", None),
        P(),
        P(),
        P(),
        P(None, ("reg", "sub")),
        P(None, ("reg", "sub")),
        P(("reg", "sub")),
    )
    out_specs = (P("grp", None, ("reg", "sub")), P(None, ("reg", "sub")))
    return jax.shard_map(local, mesh=mesh, in_specs=in_specs, out_specs=out_specs, check_vma=False)
```

```python
import jax
import jax.numpy as jnp
from jax import lax
from jax.experimental import pallas as pl
from jax.experimental.pallas import tpu as pltpu
from jax.sharding import PartitionSpec as P

LA = 90
LEV = 128
CELLS = 512
BS = 128
STEPS = 4
RUN = 4
COLS = 32
ROWS = 16
RIM = 8
EROWS = ROWS + 2 * RIM
ECOLS = COLS + 2 * RIM
BLOCK = 4 * ECOLS
BAND = 8 * ECOLS
TAG = LA
PACK = 96
THIRD = PACK // 3
EXT = BS + 4
MESH = pl.DeviceIdType.MESH
F32 = jnp.float32
BF16 = jnp.bfloat16


def exact_dot(a, b, dims):
    return lax.dot_general(
        a, b, (dims, ((), ())), precision=lax.Precision.HIGHEST, preferred_element_type=F32
    )


def fast_dot(a, b, dims):
    return lax.dot_general(a, b, (dims, ((), ())), preferred_element_type=F32)


NN = ((1,), (0,))
NT = ((1,), (1,))


def pieces(x):
    high = x.astype(BF16)
    return high, (x - high.astype(F32)).astype(BF16)


def rows8(x):
    return jnp.concatenate([x, jnp.zeros((8 - x.shape[0], x.shape[1]), x.dtype)], axis=0)


def iota(shape, dim):
    return lax.broadcasted_iota(jnp.int32, shape, dim)


def lane_roll(x, shift):
    shift = shift % x.shape[1]
    return x if shift == 0 else pltpu.roll(x, shift, 1)


def regroup(parts, n):
    width = parts[0].shape[1] // n
    group = iota(parts[0].shape, 1) // width
    out = []
    for b in range(n):
        total = lane_roll(parts[0], -b * width)
        for a in range(1, n):
            total = jnp.where(group == a, lane_roll(parts[a], (a - b) * width), total)
        out.append(total)
    return out


def body(
    n_zone,
    n_sub,
    cs_in,
    nb_in,
    mix_in,
    rate_in,
    fm_in,
    force_in,
    rm_in,
    src_in,
    rw_in,
    wet_in,
    ns_out,
    cpl_out,
    start,
    nb,
    mixing,
    rate,
    fm,
    force,
    rm,
    src,
    rw,
    wet,
    vt,
    idq,
    nidx,
    lk,
    cnt,
    vx,
    sp,
    w2,
    oh,
    fx,
    fin,
    ft,
    ftab,
    rt,
    bx,
    bin_,
    gx,
    gin,
    pbuf,
    cin,
    in_sem,
    t_send,
    t_recv,
    h_send,
    h_recv,
    f_send,
    f_recv,
    r_send,
    r_recv,
    x_send,
    x_recv,
    b_send,
    b_recv,
    g_send,
    g_recv,
):
    grp = lax.axis_index("grp")
    reg = lax.axis_index("reg")
    s = lax.axis_index("sub")
    z = reg // RUN
    j = reg % RUN
    odd = s % 2
    ocean = grp == 1
    atmos = grp == 0

    def chunk_of(place):
        return jnp.where(odd == 1, RUN - 1 - place, place)

    q = chunk_of(j)
    z_up = lax.rem(z + n_zone - 1, n_zone)
    z_down = lax.rem(z + 1, n_zone)
    s_before = lax.rem(s + n_sub - 1, n_sub)
    s_after = lax.rem(s + 1, n_sub)
    l_j = jnp.where(q == 0, j, chunk_of(q - 1))
    l_s = jnp.where(q == 0, s_before, s)
    r_j = jnp.where(q == RUN - 1, j, chunk_of(q + 1))
    r_s = jnp.where(q == RUN - 1, s_after, s)

    def at(g, zone, place, sub):
        return (g, zone * RUN + place, sub)

    run_peers = [j, j + 1 - 2 * (j % 2), lax.rem(j + 2, RUN), RUN - 1 - j]
    sub_peers = [lax.rem(s + d, n_sub) for d in range(n_sub)]
    halo_peers = [
        at(grp, z_up, j, s),
        at(grp, z_down, j, s),
        at(grp, z, l_j, l_s),
        at(grp, z, r_j, r_s),
        at(grp, z_up, l_j, l_s),
        at(grp, z_up, r_j, r_s),
        at(grp, z_down, l_j, l_s),
        at(grp, z_down, r_j, r_s),
    ]

    barrier = pltpu.get_barrier_semaphore()
    greeted = [at(grp, z, p, s) for p in run_peers[1:]]
    greeted += [at(1 - grp, z, p, s) for p in run_peers]
    greeted += [at(grp, z, j, p) for p in sub_peers[1:]]
    greeted += halo_peers
    for device in greeted:
        pl.semaphore_signal(barrier, inc=1, device_id=device, device_id_type=MESH)

    loads = [
        pltpu.make_async_copy(a, b, in_sem.at[n])
        for n, (a, b) in enumerate(
            [
                (nb_in, nb),
                (mix_in.at[0], mixing),
                (rate_in, rate),
                (fm_in, fm),
                (force_in, force),
                (rm_in, rm),
                (src_in, src),
                (rw_in, rw),
                (wet_in, wet),
            ]
        )
    ]
    columns = [
        pltpu.make_async_copy(
            cs_in.at[0, :, pl.ds(r * BS, BS)], start.at[:, pl.ds(r * BS, BS)], in_sem.at[9 + r]
        )
        for r in range(RUN)
    ]
    loads[0].start()
    for r in (3, 0, 1, 2):
        columns[r].start()
    for load in loads[1:]:
        load.start()

    lane = iota((1, LEV), 1)
    loads[0].wait()
    link = rows8(jnp.concatenate([nb[k] for k in range(3)], axis=0))
    e_row = jnp.zeros_like(link)
    for a in range(1, 8):
        e_row = e_row + (link >= a * EXT).astype(jnp.int32)
    cell = iota((8, CELLS), 1)
    offset = ECOLS * (e_row - 2 - cell // BS) + (link - e_row * EXT - 2 - cell % BS)
    offset = offset.astype(F32)

    @pl.when(ocean)
    def _():
        blocks = regroup([offset[:, r * BS : (r + 1) * BS] for r in range(RUN)], RUN)
        for c, block in enumerate(blocks):
            idq[c] = block
        for r in range(RUN):
            columns[r].wait()
            vt[r] = jnp.transpose(start[:, r * BS : (r + 1) * BS])

    @pl.when(atmos)
    def _():
        at_tag = TAG % 8
        row = iota((8, BS), 0)
        tags = pltpu.roll(offset, at_tag, 0)
        packed = None
        for r in (3, 0, 1, 2):
            columns[r].wait()
            part = slice(r * BS, (r + 1) * BS)
            mixed_rows = jnp.where(row < at_tag + 3, tags[:, part], 0.0)
            mixed_rows = jnp.where(row < at_tag, start[TAG - at_tag : PACK, part], mixed_rows)
            tall = [start[0 : TAG - at_tag, part], mixed_rows, jnp.zeros((LEV - PACK, BS), F32)]
            tall = jnp.transpose(jnp.concatenate(tall, axis=0))
            if packed is None:
                packed = tall
            else:
                tall = jnp.where(lane < PACK, tall, lane_roll(packed, PACK - r * THIRD))
            vt[r] = tall

    pl.semaphore_wait(barrier, len(greeted))

    def remote(source, target, send, recv, device):
        return pltpu.make_async_remote_copy(
            src_ref=source,
            dst_ref=target,
            send_sem=send,
            recv_sem=recv,
            device_id=device,
            device_id_type=MESH,
        )

    index_copies, state_copies, rest_copies = [], [], []
    for d in range(1, RUN):
        peer = run_peers[d]
        c = chunk_of(peer)
        there = at(grp, z, peer, s)
        index_copies.append(
            remote(idq.at[c], nidx.at[j], t_send.at[0, d], t_recv.at[0, d], there)
        )
        cells = pl.ds(pl.multiple_of(c * COLS, COLS), COLS)
        for part, copies, first, count in ((1, state_copies, 0, 3), (2, rest_copies, 3, 1)):
            copies.append(
                remote(
                    vt.at[pl.ds(first, count), cells, :],
                    vx.at[0, pl.ds(RIM + j * RUN + first, count), pl.ds(RIM, COLS)],
                    t_send.at[part, d],
                    t_recv.at[part, d],
                    there,
                )
            )

    for copy in state_copies:
        copy.start()

    @pl.when(ocean)
    def _():
        for copy in rest_copies + index_copies:
            copy.start()
        nidx[j] = idq[q]

    for r in range(RUN):
        piece = vt[r, pl.ds(pl.multiple_of(q * COLS, COLS), COLS), :]
        vx[0, RIM + j * RUN + r, RIM : RIM + COLS, :] = piece

    def halo_copies(i, rest=0, kinds=range(5)):
        first_row = RUN * i + (3 if rest else 0)
        rows = pl.ds(RIM + first_row, 1 if rest else 3)
        up = i < 2
        zone = jnp.where(up, z_up, z_down)
        landing = jnp.where(up, EROWS - RIM + first_row, first_row - RIM)
        landing = pl.ds(landing, 1 if rest else 3)
        inner, first, end = pl.ds(RIM, COLS), pl.ds(RIM, RIM), pl.ds(COLS, RIM)
        before, after = pl.ds(0, RIM), pl.ds(RIM + COLS, RIM)
        here = vx.at[0]
        routes = [
            (here.at[rows, inner], here.at[landing, inner], at(grp, zone, j, s)),
            (here.at[rows, first], here.at[landing, after], at(grp, zone, l_j, l_s)),
            (here.at[rows, end], here.at[landing, before], at(grp, zone, r_j, r_s)),
            (here.at[rows, first], here.at[rows, after], at(grp, z, l_j, l_s)),
            (here.at[rows, end], here.at[rows, before], at(grp, z, r_j, r_s)),
        ]
        return [
            remote(source, target, h_send.at[rest, kind, i], h_recv.at[rest, kind, i], device)
            for kind, (source, target, device) in enumerate(routes)
            if kind in kinds
        ]

    def send_halo(i):
        for copy in halo_copies(i):
            copy.start()

        @pl.when(ocean)
        def _():
            for copy in halo_copies(i, 1):
                copy.start()

    def await_halo(i, kinds):
        for copy in halo_copies(i, 0, kinds):
            copy.wait_recv()

        @pl.when(ocean)
        def _():
            for copy in halo_copies(i, 1, kinds):
                copy.wait_recv()

    send_halo(j)

    loads[1].wait()
    used = jnp.maximum(iota((LEV, LEV), 0), iota((LEV, LEV), 1)) < LA
    used = jnp.logical_or(used, ocean)
    m_high, m_low = pieces(jnp.where(used, jnp.transpose(mixing[...]), 0.0))
    for a in range(2):
        w2[a * LEV : (a + 1) * LEV, 0:LEV] = m_high
        w2[a * LEV : (a + 1) * LEV, LEV : 2 * LEV] = m_low

    loads[6].wait()
    place = src[...]
    owner = (place // CELLS) * RUN + (place % BS) // COLS
    inside = ((place % CELLS) // BS) * COLS + place % COLS
    for k in range(3):
        hot = (iota((BS, CELLS), 0) == inside[k : k + 1, :]).astype(F32).astype(BF16)
        oh[0:BS, k * CELLS : (k + 1) * CELLS] = hot
        oh[BS : 2 * BS, k * CELLS : (k + 1) * CELLS] = hot

    for slot, first in ((1, 0), (1, EROWS - 2), (3, 4), (3, EROWS - 6)):
        spot = slice(first * ECOLS, (first + 2) * ECOLS)
        sp[slot, spot, :] = jnp.zeros((2 * ECOLS, 2 * LEV), BF16)

    loads[2].wait()
    for d in range(1, RUN):
        state_copies[d - 1].wait_recv()

        @pl.when(ocean)
        def _(d=d):
            rest_copies[d - 1].wait_recv()

        send_halo(run_peers[d])

    gap = iota((BLOCK, BAND), 1) - iota((BLOCK, BAND), 0) - 2 * ECOLS
    gap = gap.astype(F32)

    def count(b, offsets, first):
        total = (offsets[:, first : first + 1] == gap).astype(F32)
        for k in range(1, 3):
            total = total + (offsets[:, first + k : first + k + 1] == gap).astype(F32)
        cnt[b] = total.astype(BF16)

    @pl.when(ocean)
    def _():
        for copy in index_copies:
            copy.wait_recv()
        lk[...] = jnp.zeros_like(lk)
        for i in range(RUN):
            tall = jnp.concatenate([nidx[i], jnp.zeros((BS - 8, BS), F32)], axis=0)
            tall = jnp.transpose(tall)
            for r in range(RUN):
                lk[RIM + RUN * i + r, RIM : RIM + COLS, :] = tall[r * COLS : (r + 1) * COLS]

        def one(b, carry):
            count(b, lk[pl.ds(4 * b + 2, 4)].reshape(BLOCK, LEV), 0)
            return carry

        lax.fori_loop(0, 7, one, 0)

    def count_blocks(first, end):
        @pl.when(atmos)
        def _():
            def one(b, carry):
                count(b, vx[0, pl.ds(4 * b + 2, 4)].reshape(BLOCK, LEV), TAG)
                return carry

            lax.fori_loop(first, end, one, 0)

    def unpack(first, end):
        @pl.when(atmos)
        def _():
            for g in range(first, end):
                fourth = lane_roll(vx[0, 4 * g], THIRD)
                for r in range(1, 3):
                    moved = lane_roll(vx[0, 4 * g + r], (r + 1) * THIRD + LEV - PACK - THIRD)
                    fourth = jnp.where(lane < r * THIRD, fourth, moved)
                vx[0, 4 * g + 3] = fourth

        for g in range(first, end):
            high, low = pieces(vx[0, 4 * g : 4 * g + 4].reshape(BLOCK, LEV))
            sp[0, 4 * g * ECOLS : (4 * g + 4) * ECOLS, 0:LEV] = high
            sp[0, 4 * g * ECOLS : (4 * g + 4) * ECOLS, LEV : 2 * LEV] = low

    for i in range(RUN):
        await_halo(i, (3, 4))
    unpack(2, 6)
    count_blocks(2, 5)
    for i in (2, 3):
        await_halo(i, (0, 1, 2))
    unpack(0, 2)
    count_blocks(0, 2)
    for i in (0, 1):
        await_halo(i, (0, 1, 2))
    unpack(6, 8)
    count_blocks(5, 7)

    stay = 1.0 - 3.0 * rate[...]

    def step(n, halves):
        for b in range(7):
            mine = [h for h in (0, 1) if 2 * b + h in halves]
            if not mine:
                continue
            height = 2 * len(mine)
            cells = height * ECOLS
            shift = 2 * mine[0]
            row = 4 * b + 2 + shift
            counts = cnt[b, shift * ECOLS : shift * ECOLS + cells, :]
            acc = fast_dot(counts, sp[n, 4 * b * ECOLS : 4 * b * ECOLS + BAND, :], NN)
            field = vx[n, row : row + height].reshape(cells, LEV)
            spread = stay * field + rate[...] * (acc[:, 0:LEV] + acc[:, LEV : 2 * LEV])
            high, low = pieces(spread)
            mixed = fast_dot(jnp.concatenate([high, low], axis=1), w2[...], NN)
            new = spread + (mixed[:, 0:LEV] + mixed[:, LEV : 2 * LEV])
            vx[n + 1, row : row + height] = new.reshape(height, ECOLS, LEV)
            if n < STEPS - 1:
                high, low = pieces(new)
                sp[n + 1, row * ECOLS : row * ECOLS + cells, 0:LEV] = high
                sp[n + 1, row * ECOLS : row * ECOLS + cells, LEV : 2 * LEV] = low

    n_steps = jnp.where(ocean, 1, STEPS)
    step(0, range(14))

    @pl.when(atmos)
    def _():
        for n in range(1, STEPS):
            step(n, range(n, 14 - n))

    def own(n):
        return vx[n, RIM : RIM + ROWS, RIM : RIM + COLS, :].reshape(CELLS, LEV)

    def to_owners(g, source, target, send, recv):
        return [
            remote(source.at[i], target.at[q], send.at[g, i], recv.at[j], at(g, z, i, s))
            for i in range(RUN)
        ]

    def flux_copies(g):
        return to_owners(g, fx, fin, f_send, f_recv)

    def base_copies(g):
        return to_owners(g, bx, bin_, b_send, b_recv)

    def but_own(copies, act):
        for i, copy in enumerate(copies):

            @pl.when(j != i)
            def _(copy=copy):
                act(copy)

    last = n_steps
    back_copies = []
    for d in range(1, RUN):
        peer = run_peers[d]
        back_copies.append(
            remote(
                vx.at[last, pl.ds(RIM + peer * RUN, RUN), pl.ds(RIM, COLS)],
                rt.at[:, pl.ds(pl.multiple_of(q * COLS, COLS), COLS), :],
                r_send.at[d],
                r_recv.at[d],
                at(grp, z, peer, s),
            )
        )

    loads[3].wait()

    @pl.when(atmos)
    def _():
        f_high, f_low = pieces(jnp.where(lane < LA, rows8(fm[...]) * (1.0 / STEPS), 0.0))
        v_high, v_low = pieces(own(1) + own(2) + own(3) + own(4))
        weights = jnp.concatenate([f_high, f_low], axis=0)
        flux = fast_dot(weights, v_high, NT)
        flux = flux[0:8] + flux[8:16] + fast_dot(f_high, v_low, NT)
        for i in range(RUN):
            fx[i] = flux[:, i * BS : (i + 1) * BS]
        for copy in flux_copies(1):
            copy.start()
        but_own(flux_copies(0), lambda copy: copy.start())
        fin[q] = fx[j]
        for copy in back_copies:
            copy.start()

    loads[4].wait()
    loads[5].wait()
    loads[7].wait()
    loads[8].wait()
    to_atmos = remote(gx, gin, g_send, g_recv, at(1 - grp, z, j, s))
    force_t = rows8(force[...])
    pushed_t = force_t + exact_dot(force_t, mixing[...], NT)

    @pl.when(ocean)
    def _():
        returns = rows8(rm[...])
        base = exact_dot(returns, own(1), NT)
        for i in range(RUN):
            bx[i] = base[:, i * BS : (i + 1) * BS]
        for copy in base_copies(0):
            copy.start()
        but_own(base_copies(1), lambda copy: copy.start())
        bin_[q] = bx[j]
        for copy in back_copies:
            copy.start()
        gains = jnp.zeros((8, BS), F32)
        for f in range(4):
            gain = jnp.sum(returns * pushed_t[f : f + 1, :], axis=1, keepdims=True)
            gains = jnp.where(iota((8, BS), 1) == f, gain, gains)
        gx[...] = gains
        gin[...] = gains
        to_atmos.start()

    for r in range(RUN):
        piece = vx[last, RIM + j * RUN + r, RIM : RIM + COLS, :]
        rt[r, pl.ds(pl.multiple_of(q * COLS, COLS), COLS), :] = piece

    for i in range(RUN):

        @pl.when(jnp.logical_or(ocean, j != i))
        def _(i=i):
            remote(fx.at[i], fin.at[i], f_send.at[0, i], f_recv.at[i], at(1 - grp, z, i, s)).wait_recv()

    for c in range(RUN):
        ft[c * 4 : (c + 1) * 4, :] = fin[c, 0:4, :]
    ftab[s] = ft[...]

    def over_sub(source_of, table, leg):
        return [
            remote(
                source_of(sub_peers[d]),
                table.at[s],
                x_send.at[leg, d],
                x_recv.at[leg, d],
                at(grp, z, j, sub_peers[d]),
            )
            for d in range(1, n_sub)
        ]

    gather_copies = over_sub(lambda peer: ft, ftab, 0)
    for copy in gather_copies:
        copy.start()

    for i in range(RUN):

        @pl.when(jnp.logical_or(atmos, j != i))
        def _(i=i):
            device = at(1 - grp, z, i, s)
            remote(bx.at[i], bin_.at[i], b_send.at[0, i], b_recv.at[i], device).wait_recv()

    @pl.when(atmos)
    def _():
        to_atmos.wait_recv()

    base = regroup([bin_[c] for c in range(RUN)], RUN)
    base = jnp.concatenate(base, axis=1)

    for copy in gather_copies:
        copy.wait_recv()

    n_rows = n_sub * ROWS
    high, low = pieces(ftab[...].reshape(n_rows, BS))
    table = jnp.concatenate([high, low], axis=1)
    row_owner = iota((n_rows, CELLS), 0) // 4
    ocean_flux = jnp.zeros((8, CELLS), F32)
    for k in range(3):
        taken = fast_dot(table, oh[:, k * CELLS : (k + 1) * CELLS], NN)
        taken = jnp.where(row_owner == owner[k : k + 1, :], taken, 0.0)
        taken = taken.reshape(n_rows // 8, 8, CELLS).sum(axis=0)
        ocean_flux = ocean_flux + rw[k : k + 1, :] * taken
    ocean_flux = ocean_flux + pltpu.roll(ocean_flux, 4, 0)

    wet_f = wet[...].astype(F32)
    surface = base
    for f in range(4):
        surface = surface + gin[:, f : f + 1] * ocean_flux[f : f + 1, :]
    surface = surface * wet_f
    surface = surface + pltpu.roll(surface, 4, 0)
    sums = None
    for k in range(3):
        high, low = pieces(surface * rw[k : k + 1, :])
        mine = row_owner == owner[k : k + 1, :]
        spread_out = []
        for piece in (high, low):
            tall = jnp.broadcast_to(piece.astype(F32)[None], (n_rows // 8, 8, CELLS))
            spread_out.append(jnp.where(mine, tall.reshape(n_rows, CELLS), 0.0).astype(BF16))
        part = fast_dot(
            jnp.concatenate(spread_out, axis=0), oh[0:BS, k * CELLS : (k + 1) * CELLS], NT
        )
        part = part[0:n_rows] + part[n_rows : 2 * n_rows]
        sums = part if sums is None else sums + part
    pbuf[...] = sums.reshape(n_sub, ROWS, BS)
    sum_copies = over_sub(lambda peer: pbuf.at[peer], cin, 1)
    for copy in sum_copies:
        copy.start()
    cin[s] = pbuf[s]

    for copy in back_copies:
        copy.wait_recv()

    @pl.when(atmos)
    def _():
        for r in range(RUN):
            block = jnp.transpose(rt[r])
            ns_out[0, :, r * BS : (r + 1) * BS] = jnp.where(iota((LEV, BS), 0) < LA, block, 0.0)

    @pl.when(ocean)
    def _():
        columns = jnp.transpose(jnp.concatenate([pushed_t, jnp.zeros((BS - 8, BS), F32)], axis=0))
        for r in range(RUN):
            part = slice(r * BS, (r + 1) * BS)
            forced = jnp.transpose(rt[r])
            for f in range(4):
                forced = forced + columns[:, f : f + 1] * ocean_flux[f : f + 1, part]
            old = start[:, part]
            ns_out[0, :, part] = old + wet_f[:, part] * (forced - old)

    for copy in sum_copies:
        copy.wait_recv()
    summed = cin[...].sum(axis=0)
    by_chunk = [rows8(summed[c * 4 : (c + 1) * 4, :]) for c in range(RUN)]
    for r, block in enumerate(regroup(by_chunk, RUN)):
        cpl_out[:, r * BS : (r + 1) * BS] = block[0:3, :]

    for copy in state_copies + back_copies + gather_copies + sum_copies:
        copy.wait_send()
    for i in range(RUN):
        for copy in halo_copies(i):
            copy.wait_send()

        @pl.when(ocean)
        def _(i=i):
            for copy in halo_copies(i, 1):
                copy.wait_send()


    @pl.when(atmos)
    def _():
        but_own(flux_copies(0), lambda copy: copy.wait_send())
        for copy in flux_copies(1):
            copy.wait_send()

    @pl.when(ocean)
    def _():
        to_atmos.wait_send()
        but_own(base_copies(1), lambda copy: copy.wait_send())
        for copy in base_copies(0):
            copy.wait_send()
        for copy in index_copies + rest_copies:
            copy.wait_send()


def local(
    column_state,
    neighbours,
    mixing,
    diffusivity,
    flux_map,
    force_map,
    return_map,
    sources,
    remap_weights,
    wet,
):
    n_zone = lax.axis_size("reg") // RUN
    n_sub = lax.axis_size("sub")
    vmem, dma = pltpu.VMEM, pltpu.SemaphoreType.DMA
    i32 = jnp.int32
    scratch = [
        vmem((LEV, CELLS), F32),
        vmem((3, 1, CELLS), i32),
        vmem((LEV, LEV), F32),
        vmem((1, LEV), F32),
        vmem((4, LEV), F32),
        vmem((4, LEV), F32),
        vmem((3, LEV), F32),
        vmem((3, CELLS), i32),
        vmem((3, CELLS), F32),
        vmem((1, CELLS), i32),
        vmem((RUN, BS, LEV), F32),
        vmem((RUN, 8, BS), F32),
        vmem((RUN, 8, BS), F32),
        vmem((EROWS, ECOLS, LEV), F32),
        vmem((7, BLOCK, BAND), BF16),
        vmem((STEPS + 1, EROWS, ECOLS, LEV), F32),
        vmem((STEPS + 1, EROWS * ECOLS, 2 * LEV), BF16),
        vmem((2 * LEV, 2 * LEV), BF16),
        vmem((2 * BS, 3 * CELLS), BF16),
        vmem((RUN, 8, BS), F32),
        vmem((RUN, 8, BS), F32),
        vmem((ROWS, BS), F32),
        vmem((n_sub, ROWS, BS), F32),
        vmem((RUN, BS, LEV), F32),
        vmem((RUN, 8, BS), F32),
        vmem((RUN, 8, BS), F32),
        vmem((8, BS), F32),
        vmem((8, BS), F32),
        vmem((n_sub, ROWS, BS), F32),
        vmem((n_sub, ROWS, BS), F32),
        dma((9 + RUN,)),
        dma((3, RUN)),
        dma((3, RUN)),
        dma((2, 5, RUN)),
        dma((2, 5, RUN)),
        dma((2, RUN)),
        dma((RUN,)),
        dma((RUN,)),
        dma((RUN,)),
        dma((2, n_sub)),
        dma((2, n_sub)),
        dma((2, RUN)),
        dma((RUN,)),
        dma(()),
        dma(()),
    ]

    def kernel(*refs):
        body(n_zone, n_sub, *refs)

    return pl.pallas_call(
        kernel,
        name="window",
        out_shape=(
            jax.ShapeDtypeStruct((1, LEV, CELLS), F32),
            jax.ShapeDtypeStruct((3, CELLS), F32),
        ),
        in_specs=[pl.BlockSpec(memory_space=pltpu.HBM)] * 10,
        out_specs=(pl.BlockSpec(memory_space=pltpu.VMEM),) * 2,
        scratch_shapes=scratch,
        compiler_params=pltpu.CompilerParams(
            collective_id=0, has_side_effects=True, vmem_limit_bytes=40 << 20
        ),
    )(*[pltpu.with_memory_space_constraint(a, pltpu.HBM) for a in (
        column_state,
        neighbours.transpose(1, 0, 2),
        mixing,
        diffusivity,
        flux_map,
        force_map.T,
        return_map,
        sources,
        remap_weights,
        wet.reshape(1, CELLS),
    )])


def solution(mesh):
    in_specs = (
        P("grp", None, ("reg", "sub")),
        P("grp", None, ("reg", "sub")),
        P("grp", None, None),
        P("grp", None),
        P(),
        P(),
        P(),
        P(None, ("reg", "sub")),
        P(None, ("reg", "sub")),
        P(("reg", "sub")),
    )
    out_specs = (P("grp", None, ("reg", "sub")), P(None, ("reg", "sub")))
    return jax.shard_map(local, mesh=mesh, in_specs=in_specs, out_specs=out_specs, check_vma=False)
```

```python
import jax
import jax.numpy as jnp
from jax import lax
from jax.experimental import pallas as pl
from jax.experimental.pallas import tpu as pltpu
from jax.sharding import PartitionSpec as P

LA = 90
LEV = 128
CELLS = 512
BS = 128
STEPS = 4
RUN = 4
COLS = 32
ROWS = 16
RIM = 8
EROWS = ROWS + 2 * RIM
ECOLS = COLS + 2 * RIM
BLOCK = 4 * ECOLS
BAND = 8 * ECOLS
TAG = LA
PACK = 96
THIRD = PACK // 3
EXT = BS + 4
MESH = pl.DeviceIdType.MESH
F32 = jnp.float32
BF16 = jnp.bfloat16


def exact_dot(a, b, dims):
    return lax.dot_general(
        a, b, (dims, ((), ())), precision=lax.Precision.HIGHEST, preferred_element_type=F32
    )


def fast_dot(a, b, dims):
    return lax.dot_general(a, b, (dims, ((), ())), preferred_element_type=F32)


NN = ((1,), (0,))
NT = ((1,), (1,))


def pieces(x):
    high = x.astype(BF16)
    return high, (x - high.astype(F32)).astype(BF16)


def rows8(x):
    return jnp.concatenate([x, jnp.zeros((8 - x.shape[0], x.shape[1]), x.dtype)], axis=0)


def iota(shape, dim):
    return lax.broadcasted_iota(jnp.int32, shape, dim)


def lane_roll(x, shift):
    shift = shift % x.shape[1]
    return x if shift == 0 else pltpu.roll(x, shift, 1)


def regroup(parts, n):
    width = parts[0].shape[1] // n
    group = iota(parts[0].shape, 1) // width
    out = []
    for b in range(n):
        total = lane_roll(parts[0], -b * width)
        for a in range(1, n):
            total = jnp.where(group == a, lane_roll(parts[a], (a - b) * width), total)
        out.append(total)
    return out


def body(
    n_zone,
    n_sub,
    cs_in,
    nb_in,
    mix_in,
    rate_in,
    fm_in,
    force_in,
    rm_in,
    src_in,
    rw_in,
    wet_in,
    ns_out,
    cpl_out,
    start,
    nb,
    mixing,
    rate,
    fm,
    force,
    rm,
    src,
    rw,
    wet,
    vt,
    idq,
    nidx,
    lk,
    cnt,
    vx,
    sp,
    w2,
    oh,
    fx,
    fin,
    ft,
    ftab,
    rt,
    bx,
    bin_,
    gx,
    gin,
    pbuf,
    cin,
    in_sem,
    t_send,
    t_recv,
    h_send,
    h_recv,
    f_send,
    f_recv,
    r_send,
    r_recv,
    x_send,
    x_recv,
    b_send,
    b_recv,
    g_send,
    g_recv,
):
    grp = lax.axis_index("grp")
    reg = lax.axis_index("reg")
    s = lax.axis_index("sub")
    z = reg // RUN
    j = reg % RUN
    odd = s % 2
    ocean = grp == 1
    atmos = grp == 0

    def chunk_of(place):
        return jnp.where(odd == 1, RUN - 1 - place, place)

    q = chunk_of(j)
    z_up = lax.rem(z + n_zone - 1, n_zone)
    z_down = lax.rem(z + 1, n_zone)
    s_before = lax.rem(s + n_sub - 1, n_sub)
    s_after = lax.rem(s + 1, n_sub)
    l_j = jnp.where(q == 0, j, chunk_of(q - 1))
    l_s = jnp.where(q == 0, s_before, s)
    r_j = jnp.where(q == RUN - 1, j, chunk_of(q + 1))
    r_s = jnp.where(q == RUN - 1, s_after, s)

    def at(g, zone, place, sub):
        return (g, zone * RUN + place, sub)

    run_peers = [j, j + 1 - 2 * (j % 2), lax.rem(j + 2, RUN), RUN - 1 - j]
    sub_peers = [lax.rem(s + d, n_sub) for d in range(n_sub)]
    halo_peers = [
        at(grp, z_up, j, s),
        at(grp, z_down, j, s),
        at(grp, z, l_j, l_s),
        at(grp, z, r_j, r_s),
        at(grp, z_up, l_j, l_s),
        at(grp, z_up, r_j, r_s),
        at(grp, z_down, l_j, l_s),
        at(grp, z_down, r_j, r_s),
    ]

    barrier = pltpu.get_barrier_semaphore()
    greeted = [at(grp, z, p, s) for p in run_peers[1:]]
    greeted += [at(1 - grp, z, p, s) for p in run_peers]
    greeted += [at(grp, z, j, p) for p in sub_peers[1:]]
    greeted += halo_peers
    for device in greeted:
        pl.semaphore_signal(barrier, inc=1, device_id=device, device_id_type=MESH)

    loads = [
        pltpu.make_async_copy(a, b, in_sem.at[n])
        for n, (a, b) in enumerate(
            [
                (nb_in, nb),
                (mix_in.at[0], mixing),
                (rate_in, rate),
                (fm_in, fm),
                (force_in, force),
                (rm_in, rm),
                (src_in, src),
                (rw_in, rw),
                (wet_in, wet),
            ]
        )
    ]
    columns = [
        pltpu.make_async_copy(
            cs_in.at[0, :, pl.ds(r * BS, BS)], start.at[:, pl.ds(r * BS, BS)], in_sem.at[9 + r]
        )
        for r in range(RUN)
    ]
    loads[0].start()
    for r in (3, 0, 1, 2):
        columns[r].start()
    for load in loads[1:]:
        load.start()

    lane = iota((1, LEV), 1)
    loads[0].wait()
    link = rows8(jnp.concatenate([nb[k] for k in range(3)], axis=0))
    e_row = jnp.zeros_like(link)
    for a in range(1, 8):
        e_row = e_row + (link >= a * EXT).astype(jnp.int32)
    cell = iota((8, CELLS), 1)
    offset = ECOLS * (e_row - 2 - cell // BS) + (link - e_row * EXT - 2 - cell % BS)
    offset = offset.astype(F32)

    @pl.when(ocean)
    def _():
        blocks = regroup([offset[:, r * BS : (r + 1) * BS] for r in range(RUN)], RUN)
        for c, block in enumerate(blocks):
            idq[c] = block
        for r in range(RUN):
            columns[r].wait()
            vt[r] = jnp.transpose(start[:, r * BS : (r + 1) * BS])

    @pl.when(atmos)
    def _():
        at_tag = TAG % 8
        row = iota((8, BS), 0)
        tags = pltpu.roll(offset, at_tag, 0)
        packed = None
        for r in (3, 0, 1, 2):
            columns[r].wait()
            part = slice(r * BS, (r + 1) * BS)
            mixed_rows = jnp.where(row < at_tag + 3, tags[:, part], 0.0)
            mixed_rows = jnp.where(row < at_tag, start[TAG - at_tag : PACK, part], mixed_rows)
            tall = [start[0 : TAG - at_tag, part], mixed_rows, jnp.zeros((LEV - PACK, BS), F32)]
            tall = jnp.transpose(jnp.concatenate(tall, axis=0))
            if packed is None:
                packed = tall
            else:
                tall = jnp.where(lane < PACK, tall, lane_roll(packed, PACK - r * THIRD))
            vt[r] = tall

    pl.semaphore_wait(barrier, len(greeted))

    def remote(source, target, send, recv, device):
        return pltpu.make_async_remote_copy(
            src_ref=source,
            dst_ref=target,
            send_sem=send,
            recv_sem=recv,
            device_id=device,
            device_id_type=MESH,
        )

    index_copies, state_copies, rest_copies = [], [], []
    for d in range(1, RUN):
        peer = run_peers[d]
        c = chunk_of(peer)
        there = at(grp, z, peer, s)
        index_copies.append(
            remote(idq.at[c], nidx.at[j], t_send.at[0, d], t_recv.at[0, d], there)
        )
        cells = pl.ds(pl.multiple_of(c * COLS, COLS), COLS)
        for part, copies, first, count in ((1, state_copies, 0, 3), (2, rest_copies, 3, 1)):
            copies.append(
                remote(
                    vt.at[pl.ds(first, count), cells, :],
                    vx.at[0, pl.ds(RIM + j * RUN + first, count), pl.ds(RIM, COLS)],
                    t_send.at[part, d],
                    t_recv.at[part, d],
                    there,
                )
            )

    for copy in state_copies:
        copy.start()

    @pl.when(ocean)
    def _():
        for copy in rest_copies + index_copies:
            copy.start()
        nidx[j] = idq[q]

    for r in range(RUN):
        piece = vt[r, pl.ds(pl.multiple_of(q * COLS, COLS), COLS), :]
        vx[0, RIM + j * RUN + r, RIM : RIM + COLS, :] = piece

    def halo_copies(i, rest=0, kinds=range(5)):
        first_row = RUN * i + (3 if rest else 0)
        rows = pl.ds(RIM + first_row, 1 if rest else 3)
        up = i < 2
        zone = jnp.where(up, z_up, z_down)
        landing = jnp.where(up, EROWS - RIM + first_row, first_row - RIM)
        landing = pl.ds(landing, 1 if rest else 3)
        inner, first, end = pl.ds(RIM, COLS), pl.ds(RIM, RIM), pl.ds(COLS, RIM)
        before, after = pl.ds(0, RIM), pl.ds(RIM + COLS, RIM)
        here = vx.at[0]
        routes = [
            (here.at[rows, inner], here.at[landing, inner], at(grp, zone, j, s)),
            (here.at[rows, first], here.at[landing, after], at(grp, zone, l_j, l_s)),
            (here.at[rows, end], here.at[landing, before], at(grp, zone, r_j, r_s)),
            (here.at[rows, first], here.at[rows, after], at(grp, z, l_j, l_s)),
            (here.at[rows, end], here.at[rows, before], at(grp, z, r_j, r_s)),
        ]
        return [
            remote(source, target, h_send.at[rest, kind, i], h_recv.at[rest, kind, i], device)
            for kind, (source, target, device) in enumerate(routes)
            if kind in kinds
        ]

    def send_halo(i):
        for copy in halo_copies(i):
            copy.start()

        @pl.when(ocean)
        def _():
            for copy in halo_copies(i, 1):
                copy.start()

    def await_halo(i, kinds):
        for copy in halo_copies(i, 0, kinds):
            copy.wait_recv()

        @pl.when(ocean)
        def _():
            for copy in halo_copies(i, 1, kinds):
                copy.wait_recv()

    send_halo(j)

    loads[1].wait()
    used = jnp.maximum(iota((LEV, LEV), 0), iota((LEV, LEV), 1)) < LA
    used = jnp.logical_or(used, ocean)
    m_high, m_low = pieces(jnp.where(used, jnp.transpose(mixing[...]), 0.0))
    for a in range(2):
        w2[a * LEV : (a + 1) * LEV, 0:LEV] = m_high
        w2[a * LEV : (a + 1) * LEV, LEV : 2 * LEV] = m_low

    loads[6].wait()
    place = src[...]
    owner = (place // CELLS) * RUN + (place % BS) // COLS
    inside = ((place % CELLS) // BS) * COLS + place % COLS
    for k in range(3):
        hot = (iota((BS, CELLS), 0) == inside[k : k + 1, :]).astype(F32).astype(BF16)
        oh[0:BS, k * CELLS : (k + 1) * CELLS] = hot
        oh[BS : 2 * BS, k * CELLS : (k + 1) * CELLS] = hot

    for slot, first in ((1, 0), (1, EROWS - 2), (3, 4), (3, EROWS - 6)):
        spot = slice(first * ECOLS, (first + 2) * ECOLS)
        sp[slot, spot, :] = jnp.zeros((2 * ECOLS, 2 * LEV), BF16)

    loads[2].wait()
    for d in range(1, RUN):
        state_copies[d - 1].wait_recv()

        @pl.when(ocean)
        def _(d=d):
            rest_copies[d - 1].wait_recv()

        send_halo(run_peers[d])

    gap = iota((BLOCK, BAND), 1) - iota((BLOCK, BAND), 0) - 2 * ECOLS
    gap = gap.astype(F32)

    def count(b, offsets, first):
        total = (offsets[:, first : first + 1] == gap).astype(F32)
        for k in range(1, 3):
            total = total + (offsets[:, first + k : first + k + 1] == gap).astype(F32)
        cnt[b] = total.astype(BF16)

    @pl.when(ocean)
    def _():
        for copy in index_copies:
            copy.wait_recv()
        lk[...] = jnp.zeros_like(lk)
        for i in range(RUN):
            tall = jnp.concatenate([nidx[i], jnp.zeros((BS - 8, BS), F32)], axis=0)
            tall = jnp.transpose(tall)
            for r in range(RUN):
                lk[RIM + RUN * i + r, RIM : RIM + COLS, :] = tall[r * COLS : (r + 1) * COLS]

        def one(b, carry):
            count(b, lk[pl.ds(4 * b + 2, 4)].reshape(BLOCK, LEV), 0)
            return carry

        lax.fori_loop(0, 7, one, 0)

    def count_blocks(first, end):
        @pl.when(atmos)
        def _():
            def one(b, carry):
                count(b, vx[0, pl.ds(4 * b + 2, 4)].reshape(BLOCK, LEV), TAG)
                return carry

            lax.fori_loop(first, end, one, 0)

    def unpack(first, end):
        @pl.when(atmos)
        def _():
            for g in range(first, end):
                fourth = lane_roll(vx[0, 4 * g], THIRD)
                for r in range(1, 3):
                    moved = lane_roll(vx[0, 4 * g + r], (r + 1) * THIRD + LEV - PACK - THIRD)
                    fourth = jnp.where(lane < r * THIRD, fourth, moved)
                vx[0, 4 * g + 3] = fourth

        for g in range(first, end):
            high, low = pieces(vx[0, 4 * g : 4 * g + 4].reshape(BLOCK, LEV))
            sp[0, 4 * g * ECOLS : (4 * g + 4) * ECOLS, 0:LEV] = high
            sp[0, 4 * g * ECOLS : (4 * g + 4) * ECOLS, LEV : 2 * LEV] = low

    for i in range(RUN):
        await_halo(i, (3, 4))
    unpack(2, 6)
    count_blocks(2, 5)
    for i in (2, 3):
        await_halo(i, (0, 1, 2))
    unpack(0, 2)
    count_blocks(0, 2)
    for i in (0, 1):
        await_halo(i, (0, 1, 2))
    unpack(6, 8)
    count_blocks(5, 7)

    stay = 1.0 - 3.0 * rate[...]

    def step(n, halves):
        for b in range(7):
            mine = [h for h in (0, 1) if 2 * b + h in halves]
            if not mine:
                continue
            height = 2 * len(mine)
            cells = height * ECOLS
            shift = 2 * mine[0]
            row = 4 * b + 2 + shift
            counts = cnt[b, shift * ECOLS : shift * ECOLS + cells, :]
            acc = fast_dot(counts, sp[n, 4 * b * ECOLS : 4 * b * ECOLS + BAND, :], NN)
            field = vx[n, row : row + height].reshape(cells, LEV)
            spread = stay * field + rate[...] * (acc[:, 0:LEV] + acc[:, LEV : 2 * LEV])
            high, low = pieces(spread)
            mixed = fast_dot(jnp.concatenate([high, low], axis=1), w2[...], NN)
            new = spread + (mixed[:, 0:LEV] + mixed[:, LEV : 2 * LEV])
            vx[n + 1, row : row + height] = new.reshape(height, ECOLS, LEV)
            if n < STEPS - 1:
                high, low = pieces(new)
                sp[n + 1, row * ECOLS : row * ECOLS + cells, 0:LEV] = high
                sp[n + 1, row * ECOLS : row * ECOLS + cells, LEV : 2 * LEV] = low

    n_steps = jnp.where(ocean, 1, STEPS)
    step(0, range(14))

    @pl.when(atmos)
    def _():
        for n in range(1, STEPS):
            step(n, range(n, 14 - n))

    def own(n):
        return vx[n, RIM : RIM + ROWS, RIM : RIM + COLS, :].reshape(CELLS, LEV)

    def to_owners(g, source, target, send, recv):
        return [
            remote(source.at[i], target.at[q], send.at[g, i], recv.at[j], at(g, z, i, s))
            for i in range(RUN)
        ]

    def flux_copies(g):
        return to_owners(g, fx, fin, f_send, f_recv)

    def base_copies(g):
        return to_owners(g, bx, bin_, b_send, b_recv)

    def but_own(copies, act):
        for i, copy in enumerate(copies):

            @pl.when(j != i)
            def _(copy=copy):
                act(copy)

    last = n_steps
    back_copies, back_rest = [], []
    for d in range(1, RUN):
        peer = run_peers[d]
        cells = pl.ds(pl.multiple_of(q * COLS, COLS), COLS)
        for part, copies, first, count_of in ((0, back_copies, 0, 3), (1, back_rest, 3, 1)):
            copies.append(
                remote(
                    vx.at[last, pl.ds(RIM + peer * RUN + first, count_of), pl.ds(RIM, COLS)],
                    rt.at[pl.ds(first, count_of), cells, :],
                    r_send.at[part, d],
                    r_recv.at[part, d],
                    at(grp, z, peer, s),
                )
            )

    loads[3].wait()

    @pl.when(atmos)
    def _():
        f_high, f_low = pieces(jnp.where(lane < LA, rows8(fm[...]) * (1.0 / STEPS), 0.0))
        v_high, v_low = pieces(own(1) + own(2) + own(3) + own(4))
        weights = jnp.concatenate([f_high, f_low], axis=0)
        flux = fast_dot(weights, v_high, NT)
        flux = flux[0:8] + flux[8:16] + fast_dot(f_high, v_low, NT)
        for i in range(RUN):
            fx[i] = flux[:, i * BS : (i + 1) * BS]
        for copy in flux_copies(1):
            copy.start()
        but_own(flux_copies(0), lambda copy: copy.start())
        fin[q] = fx[j]
        for g in range(RUN):
            fourth = vx[STEPS, RIM + 4 * g + 3, RIM : RIM + COLS, :]
            for r in range(3):
                kept = vx[STEPS, RIM + 4 * g + r, RIM : RIM + COLS, :]
                kept = jnp.where(lane < PACK, kept, lane_roll(fourth, PACK - r * THIRD))
                vx[STEPS, RIM + 4 * g + r, RIM : RIM + COLS, :] = kept

    loads[4].wait()
    loads[5].wait()
    loads[7].wait()
    loads[8].wait()
    to_atmos = remote(gx, gin, g_send, g_recv, at(1 - grp, z, j, s))
    force_t = rows8(force[...])
    pushed_t = force_t + exact_dot(force_t, mixing[...], NT)

    @pl.when(ocean)
    def _():
        returns = rows8(rm[...])
        base = exact_dot(returns, own(1), NT)
        for i in range(RUN):
            bx[i] = base[:, i * BS : (i + 1) * BS]
        for copy in base_copies(0):
            copy.start()
        but_own(base_copies(1), lambda copy: copy.start())
        bin_[q] = bx[j]
        for copy in back_copies + back_rest:
            copy.start()
        gains = jnp.zeros((8, BS), F32)
        for f in range(4):
            gain = jnp.sum(returns * pushed_t[f : f + 1, :], axis=1, keepdims=True)
            gains = jnp.where(iota((8, BS), 1) == f, gain, gains)
        gx[...] = gains
        gin[...] = gains
        to_atmos.start()

    for r in range(RUN):
        piece = vx[last, RIM + j * RUN + r, RIM : RIM + COLS, :]
        rt[r, pl.ds(pl.multiple_of(q * COLS, COLS), COLS), :] = piece

    for i in range(RUN):

        @pl.when(jnp.logical_or(ocean, j != i))
        def _(i=i):
            remote(fx.at[i], fin.at[i], f_send.at[0, i], f_recv.at[i], at(1 - grp, z, i, s)).wait_recv()

    for c in range(RUN):
        ft[c * 4 : (c + 1) * 4, :] = fin[c, 0:4, :]
    ftab[s] = ft[...]

    def over_sub(source_of, table, leg):
        return [
            remote(
                source_of(sub_peers[d]),
                table.at[s],
                x_send.at[leg, d],
                x_recv.at[leg, d],
                at(grp, z, j, sub_peers[d]),
            )
            for d in range(1, n_sub)
        ]

    gather_copies = over_sub(lambda peer: ft, ftab, 0)
    for copy in gather_copies:
        copy.start()

    @pl.when(atmos)
    def _():
        for copy in back_copies:
            copy.start()

    for i in range(RUN):

        @pl.when(jnp.logical_or(atmos, j != i))
        def _(i=i):
            device = at(1 - grp, z, i, s)
            remote(bx.at[i], bin_.at[i], b_send.at[0, i], b_recv.at[i], device).wait_recv()

    @pl.when(atmos)
    def _():
        to_atmos.wait_recv()

    base = regroup([bin_[c] for c in range(RUN)], RUN)
    base = jnp.concatenate(base, axis=1)

    for copy in gather_copies:
        copy.wait_recv()

    n_rows = n_sub * ROWS
    high, low = pieces(ftab[...].reshape(n_rows, BS))
    table = jnp.concatenate([high, low], axis=1)
    row_owner = iota((n_rows, CELLS), 0) // 4
    ocean_flux = jnp.zeros((8, CELLS), F32)
    for k in range(3):
        taken = fast_dot(table, oh[:, k * CELLS : (k + 1) * CELLS], NN)
        taken = jnp.where(row_owner == owner[k : k + 1, :], taken, 0.0)
        taken = taken.reshape(n_rows // 8, 8, CELLS).sum(axis=0)
        ocean_flux = ocean_flux + rw[k : k + 1, :] * taken
    ocean_flux = ocean_flux + pltpu.roll(ocean_flux, 4, 0)

    wet_f = wet[...].astype(F32)
    surface = base
    for f in range(4):
        surface = surface + gin[:, f : f + 1] * ocean_flux[f : f + 1, :]
    surface = surface * wet_f
    surface = surface + pltpu.roll(surface, 4, 0)
    sums = None
    for k in range(3):
        high, low = pieces(surface * rw[k : k + 1, :])
        mine = row_owner == owner[k : k + 1, :]
        spread_out = []
        for piece in (high, low):
            tall = jnp.broadcast_to(piece.astype(F32)[None], (n_rows // 8, 8, CELLS))
            spread_out.append(jnp.where(mine, tall.reshape(n_rows, CELLS), 0.0).astype(BF16))
        part = fast_dot(
            jnp.concatenate(spread_out, axis=0), oh[0:BS, k * CELLS : (k + 1) * CELLS], NT
        )
        part = part[0:n_rows] + part[n_rows : 2 * n_rows]
        sums = part if sums is None else sums + part
    pbuf[...] = sums.reshape(n_sub, ROWS, BS)
    sum_copies = over_sub(lambda peer: pbuf.at[peer], cin, 1)
    for copy in sum_copies:
        copy.start()
    cin[s] = pbuf[s]

    for copy in sum_copies:
        copy.wait_recv()
    summed = cin[...].sum(axis=0)
    by_chunk = [rows8(summed[c * 4 : (c + 1) * 4, :]) for c in range(RUN)]
    for r, block in enumerate(regroup(by_chunk, RUN)):
        cpl_out[:, r * BS : (r + 1) * BS] = block[0:3, :]

    for copy in back_copies:
        copy.wait_recv()

    @pl.when(atmos)
    def _():
        fourth = lane_roll(rt[0], THIRD)
        for r in range(1, 3):
            fourth = jnp.where(lane < r * THIRD, fourth, lane_roll(rt[r], (r + 1) * THIRD))
        rt[3] = fourth
        for r in range(RUN):
            block = jnp.transpose(rt[r])
            ns_out[0, :, r * BS : (r + 1) * BS] = jnp.where(iota((LEV, BS), 0) < LA, block, 0.0)

    @pl.when(ocean)
    def _():
        for copy in back_rest:
            copy.wait_recv()
        columns = jnp.transpose(jnp.concatenate([pushed_t, jnp.zeros((BS - 8, BS), F32)], axis=0))
        for r in range(RUN):
            part = slice(r * BS, (r + 1) * BS)
            forced = jnp.transpose(rt[r])
            for f in range(4):
                forced = forced + columns[:, f : f + 1] * ocean_flux[f : f + 1, part]
            old = start[:, part]
            ns_out[0, :, part] = old + wet_f[:, part] * (forced - old)

    for copy in state_copies + back_copies + gather_copies + sum_copies:
        copy.wait_send()
    for i in range(RUN):
        for copy in halo_copies(i):
            copy.wait_send()

        @pl.when(ocean)
        def _(i=i):
            for copy in halo_copies(i, 1):
                copy.wait_send()


    @pl.when(atmos)
    def _():
        but_own(flux_copies(0), lambda copy: copy.wait_send())
        for copy in flux_copies(1):
            copy.wait_send()

    @pl.when(ocean)
    def _():
        to_atmos.wait_send()
        but_own(base_copies(1), lambda copy: copy.wait_send())
        for copy in base_copies(0):
            copy.wait_send()
        for copy in index_copies + rest_copies + back_rest:
            copy.wait_send()


def local(
    column_state,
    neighbours,
    mixing,
    diffusivity,
    flux_map,
    force_map,
    return_map,
    sources,
    remap_weights,
    wet,
):
    n_zone = lax.axis_size("reg") // RUN
    n_sub = lax.axis_size("sub")
    vmem, dma = pltpu.VMEM, pltpu.SemaphoreType.DMA
    i32 = jnp.int32
    scratch = [
        vmem((LEV, CELLS), F32),
        vmem((3, 1, CELLS), i32),
        vmem((LEV, LEV), F32),
        vmem((1, LEV), F32),
        vmem((4, LEV), F32),
        vmem((4, LEV), F32),
        vmem((3, LEV), F32),
        vmem((3, CELLS), i32),
        vmem((3, CELLS), F32),
        vmem((1, CELLS), i32),
        vmem((RUN, BS, LEV), F32),
        vmem((RUN, 8, BS), F32),
        vmem((RUN, 8, BS), F32),
        vmem((EROWS, ECOLS, LEV), F32),
        vmem((7, BLOCK, BAND), BF16),
        vmem((STEPS + 1, EROWS, ECOLS, LEV), F32),
        vmem((STEPS + 1, EROWS * ECOLS, 2 * LEV), BF16),
        vmem((2 * LEV, 2 * LEV), BF16),
        vmem((2 * BS, 3 * CELLS), BF16),
        vmem((RUN, 8, BS), F32),
        vmem((RUN, 8, BS), F32),
        vmem((ROWS, BS), F32),
        vmem((n_sub, ROWS, BS), F32),
        vmem((RUN, BS, LEV), F32),
        vmem((RUN, 8, BS), F32),
        vmem((RUN, 8, BS), F32),
        vmem((8, BS), F32),
        vmem((8, BS), F32),
        vmem((n_sub, ROWS, BS), F32),
        vmem((n_sub, ROWS, BS), F32),
        dma((9 + RUN,)),
        dma((3, RUN)),
        dma((3, RUN)),
        dma((2, 5, RUN)),
        dma((2, 5, RUN)),
        dma((2, RUN)),
        dma((RUN,)),
        dma((2, RUN)),
        dma((2, RUN)),
        dma((2, n_sub)),
        dma((2, n_sub)),
        dma((2, RUN)),
        dma((RUN,)),
        dma(()),
        dma(()),
    ]

    def kernel(*refs):
        body(n_zone, n_sub, *refs)

    return pl.pallas_call(
        kernel,
        name="window",
        out_shape=(
            jax.ShapeDtypeStruct((1, LEV, CELLS), F32),
            jax.ShapeDtypeStruct((3, CELLS), F32),
        ),
        in_specs=[pl.BlockSpec(memory_space=pltpu.HBM)] * 10,
        out_specs=(pl.BlockSpec(memory_space=pltpu.VMEM),) * 2,
        scratch_shapes=scratch,
        compiler_params=pltpu.CompilerParams(
            collective_id=0, has_side_effects=True, vmem_limit_bytes=40 << 20
        ),
    )(*[pltpu.with_memory_space_constraint(a, pltpu.HBM) for a in (
        column_state,
        neighbours.transpose(1, 0, 2),
        mixing,
        diffusivity,
        flux_map,
        force_map.T,
        return_map,
        sources,
        remap_weights,
        wet.reshape(1, CELLS),
    )])


def solution(mesh):
    in_specs = (
        P("grp", None, ("reg", "sub")),
        P("grp", None, ("reg", "sub")),
        P("grp", None, None),
        P("grp", None),
        P(),
        P(),
        P(),
        P(None, ("reg", "sub")),
        P(None, ("reg", "sub")),
        P(("reg", "sub")),
    )
    out_specs = (P("grp", None, ("reg", "sub")), P(None, ("reg", "sub")))
    return jax.shard_map(local, mesh=mesh, in_specs=in_specs, out_specs=out_specs, check_vma=False)
```
